256 devices in a mesh: blk: 256 (over x, y, z, core).
Axes of the slice: x: 4, y: 4, z: 8, core: 2. Of those that a mesh axis runs over, the one named last changes fastest.
Arguments:
- right_side: float32 [32768, 128], P('blk')
- kernel_tiles: float32 [256, 129, 128, 128], P('blk'), as said below
- route_pairs: int32 [129, 2], replicated, may hold values from 0 to 30, as said below
Outputs:
- solution: float32 [32768, 128], P('blk')
- residual: float32 [32768, 128], P('blk')
The draws below stay inside these ranges and needn't reach their ends.
Inputs may be any that keep to these rules, and one draw needn't show every extreme that they name: For every row t, cover[route_pairs[t,1]] - cover[route_pairs[t,0]] is congruent to t modulo 256, with cover as in the reference program. kernel_tiles makes K symmetric with a positive diagonal of about 1 to 16 inside the diagonal tiles; K is positive definite.
All inputs are finite; a program needn't handle non-finite values.
Results may differ from the reference program's by a relative error of at most 0.0003.
Values sent between devices are 32-bit elements; how exact they have to be, the bound alone decides.
A program may use at most 128 MiB of HBM per device.

```python
import math
import jax
import jax.numpy as jnp
import numpy as np
from jax import lax

B = 128
R = 128
ITERS = 1
NB = 256
N = 32768
NT = 129
SPAN = 16


def draw_right_side(key, part):
    rows = jnp.arange(N, dtype=jnp.int32) // B
    factor = 0.6 + 1.2 * rows.astype(jnp.float32) / (NB - 1)
    values = jnp.clip(jax.random.normal(key, (N, R), jnp.float32), -6.0, 6.0)
    return values * factor[:, None]


def draw_kernel_tiles(key, part):
    entry_scale = 0.52 / math.sqrt(N)
    first_key = jax.random.fold_in(key, 11)
    second_key = jax.random.fold_in(key, 12)
    entries = jax.random.uniform(first_key, (NB, NT, B, B), jnp.float32, -entry_scale, entry_scale)
    ridge = jnp.exp(jax.random.uniform(second_key, (NB, B), jnp.float32, 0.0, math.log(4.0)))
    center = entries[:, 0]
    center = 0.5 * (center + jnp.swapaxes(center, 1, 2)) + ridge[:, :, None] * jnp.eye(B, dtype=jnp.float32)[None]
    upper = entries[:, NT - 1]
    flipped = jnp.swapaxes(jnp.roll(upper, NB // 2, axis=0), 1, 2)
    owner_ids = jnp.arange(NB, dtype=jnp.int32)[:, None, None]
    far_tile = jnp.where(owner_ids >= NB // 2, flipped, upper)
    return entries.at[:, 0].set(center).at[:, NT - 1].set(far_tile)


def draw_route_pairs(key, part):
    cover_set = np.array([k for k in range(SPAN)] + [k * SPAN for k in range(1, NB // SPAN)], dtype=np.int64)
    cover_len = cover_set.shape[0]
    distance = (cover_set[None, :] - cover_set[:, None]) % NB
    distances = jnp.array(distance.reshape(-1), dtype=jnp.int32)
    scores = jax.random.randint(key, (NT, cover_len * cover_len), 0, 1 << 20) * (cover_len * cover_len)
    scores = scores + jnp.arange(cover_len * cover_len, dtype=jnp.int32)[None, :]
    usable = distances[None, :] == jnp.arange(NT, dtype=jnp.int32)[:, None]
    scores = jnp.where(usable, scores, -1)
    _, chosen = lax.top_k(scores, 1)
    chosen = chosen[:, 0].astype(jnp.int32)
    return jnp.stack([chosen // cover_len, chosen % cover_len], axis=1).astype(jnp.int32)


def setup_inputs(seed: int = 0) -> dict:
    key_of = jax.random.split(jax.random.key(seed), 4)
    return {
        "right_side": draw_right_side(jax.random.fold_in(key_of[3], 71), 0),
        "kernel_tiles": draw_kernel_tiles(jax.random.fold_in(key_of[3], 71), 0),
        "route_pairs": draw_route_pairs(jax.random.fold_in(key_of[3], 71), 0),
    }


def cover_offsets():
    return [k for k in range(SPAN)] + [k * SPAN for k in range(1, NB // SPAN)]


def apply_kernel(kernel_tiles, route_pairs, vector):
    cover_set = jnp.array(cover_offsets(), dtype=jnp.int32)
    row_off = cover_set[route_pairs[:, 0]]
    col_off = cover_set[route_pairs[:, 1]]
    slot_ids = jnp.arange(NT, dtype=jnp.int32)
    mirror = ((slot_ids > 0) & (slot_ids < NT - 1)).astype(vector.dtype)

    def visit_owner(summed, entry_pair):
        tile_set, owner_id = entry_pair
        row_blk = ((owner_id + row_off) % NB).astype(jnp.int32)
        col_blk = ((owner_id + col_off) % NB).astype(jnp.int32)
        by_row = jnp.einsum("tij,tjr->tir", tile_set, vector[col_blk], precision=lax.Precision.HIGHEST)
        by_col = jnp.einsum("tji,tjr->tir", tile_set, vector[row_blk], precision=lax.Precision.HIGHEST)
        by_col = by_col * mirror[:, None, None]
        summed = summed.at[row_blk].add(by_row).at[col_blk].add(by_col)
        return summed, None

    summed, _ = lax.scan(visit_owner, jnp.zeros_like(vector), (kernel_tiles, jnp.arange(NB, dtype=jnp.int32)))
    return summed


def reference(right_side, kernel_tiles, route_pairs):
    rhs_blocks = right_side.reshape(NB, B, R)
    solution = jnp.zeros_like(rhs_blocks)
    residual = rhs_blocks
    direction = rhs_blocks
    norm_now = jnp.sum(residual * residual, axis=(0, 1))
    for step in range(ITERS):
        image = apply_kernel(kernel_tiles, route_pairs, direction)
        step_len = norm_now / jnp.sum(direction * image, axis=(0, 1))
        solution = solution + step_len * direction
        residual = residual - step_len * image
        norm_next = jnp.sum(residual * residual, axis=(0, 1))
        direction = residual + (norm_next / norm_now) * direction
        norm_now = norm_next
    return solution.reshape(N, R), residual.reshape(N, R)
```

```python
import functools

import jax
import jax.numpy as jnp
from jax import lax
from jax.experimental import pallas as pl
from jax.experimental.pallas import tpu as pltpu
from jax.sharding import PartitionSpec as P

MESH = pl.DeviceIdType.MESH
NB = 256
B = 128
NT = 129
NC = 31
CHUNKS = 8
HALF = B // 2
F32 = jnp.float32
BF16 = jnp.bfloat16


def split_pair(value):
    high = value.astype(BF16)
    low = (value - high.astype(F32)).astype(BF16)
    return high, low


def cg_kernel(
    rp, x_ref, tiles, sol_ref, res_ref,
    tf, tb, xs, wb, part, prods, rel_in, cross_in, axis_in, half_a, half_b, v_out, v_mid, v_near, v_far,
    tile_sem, g_send, g_recv, c_send, c_recv, ax_send, ax_recv, ha_send, ha_recv, hb_send, hb_recv,
    s_send, s_recv, d_send, d_recv, ox_send, ox_recv, pa_send, pa_recv, pb_send, pb_recv,
    n_send, n_recv, f_send, f_recv,
):
    me = lax.axis_index("blk")
    par = lax.rem(me, 2)
    partner = me + 1 - 2 * par
    col = me // 16
    px = me // 64
    py = lax.rem(col, 4)

    def near(step):
        return lax.rem(me + step + NB, NB)

    def at_x(step):
        return me + (lax.rem(px + step, 4) - px) * 64

    def at_y(step):
        return me + (lax.rem(py + step, 4) - py) * 16

    def slot(dx, dy, tx, ty):
        owner_col = lax.rem(px + dx, 4) * 4 + lax.rem(py + dy, 4)
        there_col = lax.rem(px + tx, 4) * 4 + lax.rem(py + ty, 4)
        return 15 + lax.rem(owner_col - there_col + 16, 16)

    def remote(src, dst, send_sem, recv_sem, device):
        return pltpu.make_async_remote_copy(
            src_ref=src, dst_ref=dst, send_sem=send_sem, recv_sem=recv_sem,
            device_id=(device,), device_id_type=MESH,
        )

    bounds = [NT * q // CHUNKS for q in range(CHUNKS + 1)]
    tile_copies = []
    for q in range(CHUNKS):
        span = pl.ds(bounds[q], bounds[q + 1] - bounds[q])
        copy = pltpu.make_async_copy(tiles.at[0, span], tf.at[span], tile_sem.at[q])
        copy.start()
        tile_copies.append(copy)

    barrier = pltpu.get_barrier_semaphore()
    axis_devices = [at_x(d) for d in (1, 2, 3)] + [at_y(d) for d in (1, 2, 3)]
    for device in axis_devices + [near(2), near(4), near(12), near(14), near(-2), partner]:
        pl.semaphore_signal(barrier, inc=1, device_id=(device,), device_id_type=MESH)
    pl.semaphore_wait(barrier, 12)

    sends = []

    def go(copy):
        copy.start()
        sends.append(copy)

    for d in (1, 2, 3):
        go(remote(x_ref, xs.at[slot(0, 0, 0, d)], ax_send.at[2 + d], ax_recv.at[2 + d], at_y(d)))
        go(remote(x_ref, xs.at[slot(0, 0, d, 0)], ax_send.at[d - 1], ax_recv.at[d - 1], at_x(d)))
    for r in (2, 4, 14, 12):
        go(remote(x_ref, xs.at[r], g_send.at[r // 2 - 1], g_recv.at[r // 2 - 1], near(-r)))
    xs[0] = x_ref[...]

    def split_tile(t, carry):
        value = tf[t]
        high, low = split_pair(value)
        tb[t, 0, :, 0:B] = high
        tb[t, 0, :, B : 2 * B] = low
        high, low = split_pair(value.T)
        tb[t, 1, :, 0:B] = high
        tb[t, 1, :, B : 2 * B] = low
        return carry

    def prepare(q):
        tile_copies[q].wait()
        lax.fori_loop(bounds[q], bounds[q + 1], split_tile, 0)

    def arrive_near(r):
        remote(x_ref, xs.at[r], g_send.at[r // 2 - 1], g_recv.at[r // 2 - 1], near(-r)).wait_recv()

    def cross(r):
        place = r // 2 - 1 + par
        go(remote(xs.at[r], xs.at[r - 1 + 2 * par], c_send.at[place], c_recv.at[place], partner))

    for q in range(4):
        prepare(q)

    arrive_near(4)
    go(remote(xs.at[4], xs.at[6], g_send.at[2], g_recv.at[2], near(-2)))
    go(remote(xs.at[4], xs.at[8], g_send.at[3], g_recv.at[3], near(-4)))
    arrive_near(12)
    go(remote(xs.at[12], xs.at[10], g_send.at[4], g_recv.at[4], near(2)))
    for e in (1, 2, 3):
        src = slot(e, 0, 0, 0)
        remote(x_ref, xs.at[src], ax_send.at[3 - e], ax_recv.at[3 - e], partner).wait_recv()
        for d in (1, 2, 3):
            place = 3 * (e - 1) + d - 1
            rows = pl.ds(0, HALF)
            go(remote(xs.at[src, rows], xs.at[slot(e, 0, 0, d), rows], ha_send.at[place], ha_recv.at[place], at_y(d)))
        src = slot(0, e, 0, 0)
        remote(x_ref, xs.at[src], ax_send.at[6 - e], ax_recv.at[6 - e], partner).wait_recv()
        for d in (1, 2, 3):
            place = 3 * (e - 1) + d - 1
            rows = pl.ds(HALF, HALF)
            go(remote(xs.at[src, rows], xs.at[slot(0, e, d, 0), rows], hb_send.at[place], hb_recv.at[place], at_x(d)))
    for r in (4, 12):
        cross(r)
    for r in (2, 14):
        arrive_near(r)
        cross(r)
    for q in range(4, CHUNKS):
        prepare(q)
    for r in (6, 10, 8):
        arrive_near(r)
        cross(r)
    for e in (1, 2, 3):
        for d in (1, 2, 3):
            place = 3 * (e - 1) + d - 1
            rows = pl.ds(0, HALF)
            dst = xs.at[slot(e, 4 - d, 0, 0), rows]
            remote(dst, dst, ha_send.at[place], ha_recv.at[place], partner).wait_recv()
            rows = pl.ds(HALF, HALF)
            dst = xs.at[slot(4 - d, e, 0, 0), rows]
            remote(dst, dst, hb_send.at[place], hb_recv.at[place], partner).wait_recv()
    go(remote(xs.at[16 - 16 * par], xs.at[15 - 14 * par], c_send.at[7 - 7 * par], c_recv.at[7 - 7 * par], partner))
    for i in range(8):
        dst = xs.at[2 * i + 1]
        remote(dst, dst, c_send.at[i], c_recv.at[i], partner).wait_recv()

    def split_block(c, carry):
        high, low = split_pair(xs[c])
        wb[c, 0:B, 0:B] = high
        wb[c, 0:B, B : 2 * B] = low
        wb[c, B : 2 * B, 0:B] = high
        wb[c, B : 2 * B, B : 2 * B] = low
        return carry

    lax.fori_loop(0, NC, split_block, 0)

    def product(t, turn, c):
        both = jnp.dot(tb[t, turn], wb[c], preferred_element_type=F32)
        return both[:, 0:B] + both[:, B : 2 * B]

    def near_tile(i, carry):
        for u in range(3):
            place = 3 * i + u
            t = jnp.where(place < 16, place, 16 * (place - 15))
            prods[place, 0] = product(t, 0, rp[t, 1])
            prods[place, 1] = product(t, 1, rp[t, 0])
        return carry

    lax.fori_loop(0, 8, near_tile, 0)

    def as_mask(flag):
        return flag.astype(jnp.int32).astype(F32)

    def place_all(c, carry):
        part[c] = as_mask(rp[0, 0] == c) * prods[0, 0]
        return carry

    lax.fori_loop(0, NC, place_all, 0)

    def place_small(c, carry):
        total = part[c]
        for u in range(16):
            by_row = u < 16 - c
            t = jnp.where(by_row, u + 1, u + c - 15)
            safe = jnp.minimum(t, 15)
            start = rp[safe, 0]
            hit = jnp.where(by_row, start, start + safe) == c
            mask = as_mask(hit) * as_mask(t < 16)
            total = total + mask * prods[safe, jnp.where(by_row, 0, 1)]
        part[c] = total
        return carry

    lax.fori_loop(0, 17, place_small, 0)

    def place_large(l, carry):
        c = jnp.where(l == 0, 0, 15 + l)
        total = part[c]
        for m in range(1, 9):
            total = total + as_mask(rp[16 * m, 0] == c) * prods[15 + m, 0]
            if m < 8:
                total = total + as_mask(rp[16 * m, 1] == c) * prods[15 + m, 1]
        part[c] = total
        return carry

    lax.fori_loop(0, 16, place_large, 0)

    def far_tiles(j, carry):
        first = jnp.zeros((B, B), F32)
        second = jnp.zeros((B, B), F32)
        for k in range(2, 9):
            t = 16 * k - j
            ahead = rp[t, 0] == j
            small = jnp.where(ahead, j, 16 - j)
            large = jnp.where(ahead, 15 + k, 32 - k)
            turn = jnp.where(ahead, 0, 1)
            mask = as_mask(ahead)
            to_small = product(t, turn, large)
            to_large = product(t, 1 - turn, small)
            kept = mask * to_small
            first = first + kept
            second = second + (1.0 - mask) * to_small
            part[15 + k] += mask * to_large
            part[32 - k] += (1.0 - mask) * to_large
        part[j] += first
        part[16 - j] += second
        return carry

    lax.fori_loop(1, 16, far_tiles, 0)

    def fold_rows(value):
        total = value[0:8]
        for q in range(1, B // 8):
            total = total + value[8 * q : 8 * q + 8]
        return total

    def add_inner(c, carry):
        return carry + fold_rows(xs[c] * part[c])

    inner = lax.fori_loop(0, NC, add_inner, jnp.zeros((8, B), F32))
    own = x_ref[...]
    norm = jnp.sum(fold_rows(own * own), axis=0, keepdims=True)
    inner = jnp.sum(inner, axis=0, keepdims=True)
    row_ids = lax.broadcasted_iota(jnp.int32, (8, B), 0)
    v_out[...] = jnp.where(row_ids == 0, inner, jnp.where(row_ids == 1, norm, 0.0))
    for k in range(1, 16):
        go(remote(v_out, v_near.at[k - 1], n_send.at[k - 1], n_recv.at[k - 1], near(k)))

    for i in range(8):
        go(remote(part.at[2 * i + 1], cross_in.at[i], ox_send.at[i], ox_recv.at[i], partner))
    def send_halves(e, d):
        place = 3 * (e - 1) + d - 1
        rows = pl.ds(0, HALF)
        go(remote(part.at[slot(e, d, 0, 0), rows], half_a.at[place], pa_send.at[place], pa_recv.at[place], at_y(d)))
        rows = pl.ds(HALF, HALF)
        go(remote(part.at[slot(d, e, 0, 0), rows], half_b.at[place], pb_send.at[place], pb_recv.at[place], at_x(d)))

    for e in (1, 2, 3):
        for d in (1, 2, 3):
            if e + d > 2:
                send_halves(e, d)
    for i in range(8):
        remote(cross_in.at[i], cross_in.at[i], ox_send.at[i], ox_recv.at[i], partner).wait_recv()

    def merge(i):
        c = 2 * i + 2 - 2 * par
        part[c] += cross_in[i]

    def add_cross(i, carry):
        merge(i)
        return carry

    lax.fori_loop(0, 8, add_cross, 0)
    send_halves(1, 1)
    go(remote(part.at[8], rel_in.at[0], s_send.at[0], s_recv.at[0], near(4)))
    go(remote(part.at[6], rel_in.at[1], s_send.at[1], s_recv.at[1], near(2)))
    go(remote(part.at[10], rel_in.at[2], s_send.at[2], s_recv.at[2], near(-2)))
    go(remote(part.at[2], rel_in.at[3], s_send.at[3], s_recv.at[3], near(2)))
    go(remote(part.at[14], rel_in.at[4], s_send.at[4], s_recv.at[4], near(14)))

    for k in range(15):
        remote(v_out, v_near.at[k], n_send.at[k], n_recv.at[k], partner).wait_recv()
    mid = v_out[...]
    for k in range(15):
        mid = mid + v_near[k]
    v_mid[...] = mid
    for k in range(1, 16):
        go(remote(v_mid, v_far.at[k - 1], f_send.at[k - 1], f_recv.at[k - 1], near(16 * k)))

    for e in (1, 2, 3):
        at = slot(e, 0, 0, 0)
        for d in (1, 2, 3):
            place = 3 * (e - 1) + d - 1
            remote(half_a.at[place], half_a.at[place], pa_send.at[place], pa_recv.at[place], partner).wait_recv()
            part[at, 0:HALF] += half_a[place]
        go(remote(part.at[at], axis_in.at[e - 1], d_send.at[e - 1], d_recv.at[e - 1], at_x(e)))
        at = slot(0, e, 0, 0)
        for d in (1, 2, 3):
            place = 3 * (e - 1) + d - 1
            remote(half_b.at[place], half_b.at[place], pb_send.at[place], pb_recv.at[place], partner).wait_recv()
            part[at, HALF:B] += half_b[place]
        go(remote(part.at[at], axis_in.at[2 + e], d_send.at[2 + e], d_recv.at[2 + e], at_y(e)))
    for i in range(3):
        remote(rel_in.at[i], rel_in.at[i], s_send.at[i], s_recv.at[i], partner).wait_recv()
    part[4] += rel_in[0] + rel_in[1]
    go(remote(part.at[4], rel_in.at[5], s_send.at[5], s_recv.at[5], near(4)))
    part[12] += rel_in[2]
    go(remote(part.at[12], rel_in.at[6], s_send.at[6], s_recv.at[6], near(12)))

    for k in range(15):
        remote(v_mid, v_far.at[k], f_send.at[k], f_recv.at[k], partner).wait_recv()
    total = v_mid[...]
    for k in range(15):
        total = total + v_far[k]
    step = total[1:2] / total[0:1]

    for i in range(3, 7):
        remote(rel_in.at[i], rel_in.at[i], s_send.at[i], s_recv.at[i], partner).wait_recv()
    for i in range(6):
        remote(axis_in.at[i], axis_in.at[i], d_send.at[i], d_recv.at[i], partner).wait_recv()
    image = part[0]
    for i in range(3, 7):
        image = image + rel_in[i]
    for i in range(6):
        image = image + axis_in[i]
    sol_ref[...] = step * own
    res_ref[...] = own - step * image
    for copy in sends:
        copy.wait_send()


def per_device(right_side, kernel_tiles, route_pairs):
    vmem = pltpu.VMEM
    dma = pltpu.SemaphoreType.DMA
    counts = [7, 8, 6, 9, 9, 7, 6, 8, 9, 9, 15, 15]
    sems = []
    for count in counts:
        sems += [dma((count,)), dma((count,))]
    out = jax.ShapeDtypeStruct((B, B), F32)
    whole = pl.BlockSpec(memory_space=vmem)
    return pl.pallas_call(
        cg_kernel,
        out_shape=(out, out),
        in_specs=[pl.BlockSpec(memory_space=pltpu.SMEM), whole, pl.BlockSpec(memory_space=pl.ANY)],
        out_specs=(whole, whole),
        scratch_shapes=[
            vmem((NT, B, B), F32),
            vmem((NT, 2, B, 2 * B), BF16),
            vmem((NC, B, B), F32),
            vmem((NC, 2 * B, 2 * B), BF16),
            vmem((NC, B, B), F32),
            vmem((24, 2, B, B), F32),
            vmem((7, B, B), F32),
            vmem((8, B, B), F32),
            vmem((6, B, B), F32),
            vmem((9, HALF, B), F32),
            vmem((9, HALF, B), F32),
            vmem((8, B), F32),
            vmem((8, B), F32),
            vmem((15, 8, B), F32),
            vmem((15, 8, B), F32),
            dma((CHUNKS,)),
        ]
        + sems,
        compiler_params=pltpu.CompilerParams(
            collective_id=0, has_side_effects=True, vmem_limit_bytes=60 * 1024 * 1024
        ),
    )(route_pairs, right_side, kernel_tiles)


def solution(mesh):
    return jax.shard_map(
        per_device,
        mesh=mesh,
        in_specs=(P("blk", None), P("blk", None, None, None), P()),
        out_specs=(P("blk", None), P("blk", None)),
        check_vma=False,
    )
```

```python
import functools

import jax
import jax.numpy as jnp
from jax import lax
from jax.experimental import pallas as pl
from jax.experimental.pallas import tpu as pltpu
from jax.sharding import PartitionSpec as P

MESH = pl.DeviceIdType.MESH
NB = 256
B = 128
NT = 129
NC = 31
CHUNK = 16
CHUNKS = 9
HALF = B // 2
F32 = jnp.float32
BF16 = jnp.bfloat16


def split_pair(value):
    high = value.astype(BF16)
    low = (value - high.astype(F32)).astype(BF16)
    return high, low


def sort_network(count):
    pairs = []
    p = 1
    while p < count:
        k = p
        while k >= 1:
            for j in range(k % p, count - k, 2 * k):
                for i in range(min(k, count - j - k)):
                    if (i + j) // (2 * p) == (i + j + k) // (2 * p):
                        pairs.append((i + j, i + j + k))
            k //= 2
        p *= 2
    return pairs


def cg_kernel(
    rp, x_ref, tiles, image_ref, step_ref,
    tf, tb, xs, wb, part, wide, tight, wide_runs, tight_runs,
    cross_in, relay_in, near_in, axis_in, half_a, half_b,
    v_out, v_mid, v_near, v_far, wide_keys, tight_keys, wide_last, tight_last,
    tile_sem, sent, g_recv, first_recv, block_recv, cross_recv, back_recv, relay_recv, half_recv, end_recv, sum_recv,
):
    me = lax.axis_index("blk")
    par = lax.rem(me, 2)
    partner = me + 1 - 2 * par
    col = me // 16
    px = me // 64
    py = lax.rem(col, 4)

    def near(step):
        return lax.rem(me + step + NB, NB)

    def at_x(step):
        return me + (lax.rem(px + step, 4) - px) * 64

    def at_y(step):
        return me + (lax.rem(py + step, 4) - py) * 16

    def slot(dx, dy, tx, ty):
        owner_col = lax.rem(px + dx, 4) * 4 + lax.rem(py + dy, 4)
        there_col = lax.rem(px + tx, 4) * 4 + lax.rem(py + ty, 4)
        return 15 + lax.rem(owner_col - there_col + 16, 16)

    def remote(src, dst, send_sem, recv_sem, device):
        return pltpu.make_async_remote_copy(
            src_ref=src, dst_ref=dst, send_sem=send_sem, recv_sem=recv_sem,
            device_id=(device,), device_id_type=MESH,
        )

    def arrive(dst, recv_sem):
        remote(dst, dst, sent.at[0], recv_sem, partner).wait_recv()

    half = [pl.ds(0, HALF), pl.ds(HALF, HALF)]
    low_half, high_half = half
    halves_sent = [0] * 8

    def go(group, halves, src, dst, recv_sem, device):
        halves_sent[group] += halves
        remote(src, dst, sent.at[group], recv_sem, device).start()

    def tile_copy(q, count):
        span = pl.ds(q * CHUNK, count)
        return pltpu.make_async_copy(tiles.at[0, span], tf.at[span], tile_sem.at[q])

    for q in range(CHUNKS - 1):
        tile_copy(q, CHUNK).start()
    tile_copy(CHUNKS - 1, 1).start()

    barrier = pltpu.get_barrier_semaphore()
    axis_devices = [at_x(d) for d in (1, 2, 3)] + [at_y(d) for d in (1, 2, 3)]
    for device in axis_devices + [near(2), near(4), near(12), near(14), near(-2), partner]:
        pl.semaphore_signal(barrier, inc=1, device_id=(device,), device_id_type=MESH)
    def ordered(keys, count):
        keys = list(keys)
        for lower, upper in sort_network(count):
            if upper < len(keys):
                small, big = jnp.minimum(keys[lower], keys[upper]), jnp.maximum(keys[lower], keys[upper])
                keys[lower], keys[upper] = small, big
        return keys

    keys = [rp[0, 16 * m] * 32 + m - 1 for m in range(1, 9)]
    keys += [rp[1, 16 * m] * 32 + m + 7 for m in range(1, 8)]
    for i, key in enumerate(ordered(keys, 16)):
        wide_keys[i] = key
    keys = [rp[0, t] * 32 + t for t in range(16)] + [rp[1, t] * 32 + t + 15 for t in range(1, 16)]
    for i, key in enumerate(ordered(keys, 32)):
        tight_keys[i] = key

    def find_last(c, carry):
        for keys, last, count in ((wide_keys, wide_last, 15), (tight_keys, tight_last, 31)):
            found = jnp.int32(-1)
            for i in range(count):
                found = found + (keys[i] < (c + 1) * 32).astype(jnp.int32)
            ends_here = lax.div(keys[jnp.maximum(found, 0)], 32) == c
            last[c] = jnp.where(ends_here, found, count)
        return carry

    lax.fori_loop(0, NC, find_last, 0)

    pl.semaphore_wait(barrier, 12)

    def first_x(d, h):
        sem = first_recv.at[d - 1] if h == 0 else block_recv
        go(0, 1, x_ref.at[half[h]], xs.at[slot(0, 0, d, 0), half[h]], sem, at_x(d))

    def first_y(d, h):
        sem = first_recv.at[2 + d] if h == 1 else block_recv
        go(0, 1, x_ref.at[half[h]], xs.at[slot(0, 0, 0, d), half[h]], sem, at_y(d))

    for h in (0, 1):
        go(1, 1, x_ref.at[half[h]], xs.at[4, half[h]], g_recv.at[h], near(-4))
        go(1, 1, x_ref.at[half[h]], xs.at[12, half[h]], g_recv.at[2 + h], near(-12))
    for d in (2, 1, 3):
        first_x(d, 0)
        first_y(d, 1)
    xs[0] = x_ref[...]

    def split_tile(t):
        high, low = split_pair(tf[t])
        tb[t, 0, :, 0:B] = high
        tb[t, 0, :, B : 2 * B] = low
        tb[t, 1, :, 0:B] = high.T
        tb[t, 1, :, B : 2 * B] = low.T

    def prepare(q, carry):
        tile_copy(q, CHUNK).wait()
        for u in range(CHUNK):
            split_tile(q * CHUNK + u)
        return carry

    def cross(r):
        go(2, 2, xs.at[r], xs.at[r - 1 + 2 * par], cross_recv, partner)

    lax.fori_loop(0, 3, prepare, 0)
    go(1, 2, x_ref, xs.at[2], g_recv.at[4], near(-2))
    go(1, 2, x_ref, xs.at[14], g_recv.at[5], near(-14))
    for d in (1, 3, 2):
        first_x(d, 1)
        first_y(d, 0)
    lax.fori_loop(3, CHUNKS - 1, prepare, 0)
    tile_copy(CHUNKS - 1, 1).wait()
    split_tile(NT - 1)

    def forward(e):
        src = slot(e, 0, 0, 0)
        arrive(xs.at[src, low_half], first_recv.at[3 - e])
        for d in (2, 1, 3):
            go(3, 1, xs.at[src, low_half], xs.at[slot(e, 0, 0, d), low_half], block_recv, at_y(d))
        src = slot(0, e, 0, 0)
        arrive(xs.at[src, high_half], first_recv.at[6 - e])
        for d in (2, 1, 3):
            go(3, 1, xs.at[src, high_half], xs.at[slot(0, e, d, 0), high_half], block_recv, at_x(d))

    def forward_near(h):
        arrive(xs.at[4, half[h]], g_recv.at[h])
        go(1, 1, xs.at[4, half[h]], xs.at[8, half[h]], g_recv.at[6], near(-4))
        go(1, 1, xs.at[4, half[h]], xs.at[6, half[h]], g_recv.at[7], near(-2))
        arrive(xs.at[12, half[h]], g_recv.at[2 + h])
        go(1, 1, xs.at[12, half[h]], xs.at[10, half[h]], g_recv.at[8], near(2))

    forward(1)
    forward(3)
    forward_near(0)
    forward(2)
    forward_near(1)
    for r in (4, 12):
        cross(r)
    for r, q in ((2, 4), (14, 5)):
        arrive(xs.at[r], g_recv.at[q])
        cross(r)

    def split_block(c, carry):
        high, low = split_pair(xs[c])
        wb[c, 0:B, 0:B] = high
        wb[c, 0:B, B : 2 * B] = low
        wb[c, B : 2 * B, 0:B] = high
        wb[c, B : 2 * B, B : 2 * B] = low
        return carry

    def product(t, turn, c):
        both = jnp.dot(tb[t, turn], wb[c], preferred_element_type=F32)
        return both[:, 0:B] + both[:, B : 2 * B]

    def as_mask(flag):
        return flag.astype(jnp.int32).astype(F32)

    zero = jnp.zeros((B, B), F32)

    def run_sums(keys, products, runs, count):
        total = zero
        for i in range(count):
            key = keys[i]
            before = keys[max(i - 1, 0)]
            total = as_mask(lax.div(before, 32) == lax.div(key, 32)) * total + products[lax.rem(key, 32)]
            runs[i] = total
        runs[count] = zero

    def orient(t, j, k):
        ahead = rp[0, t] == j
        small = jnp.where(ahead, j, 16 - j)
        large = jnp.where(ahead, 15 + k, 32 - k)
        return jnp.where(ahead, 0, 1), small, large, as_mask(ahead)

    def far_to_small(i, carry):
        for u in range(3):
            j = 3 * i + u + 1
            first, second = zero, zero
            for k in range(2, 9):
                turn, _, large, mask = orient(16 * k - j, j, k)
                value = product(16 * k - j, turn, large)
                first = first + mask * value
                second = second + (1.0 - mask) * value
            part[j] += first
            part[16 - j] += second
        return carry

    def far_to_large(k):
        first, second = zero, zero
        for j in range(1, 16):
            turn, small, _, mask = orient(16 * k - j, j, k)
            value = product(16 * k - j, 1 - turn, small)
            first = first + mask * value
            second = second + (1.0 - mask) * value
        for c, value in ((15 + k, first), (32 - k, second)):
            part[c] = value + wide_runs[wide_last[c]] + tight_runs[tight_last[c]]

    def far_pair(i, carry):
        far_to_large(2 * i + 1)
        far_to_large(2 * i + 2)
        return carry

    arrive(xs.at[pl.ds(17, 12)], block_recv)
    go(2, 2, xs.at[16 - 16 * par], xs.at[15 - 14 * par], cross_recv, partner)
    split_block(0, 0)
    lax.fori_loop(16, NC, split_block, 0, unroll=5)

    for m in range(1, 9):
        wide[m - 1] = product(16 * m, 0, rp[1, 16 * m])
        if m < 8:
            wide[m + 7] = product(16 * m, 1, rp[0, 16 * m])
    run_sums(wide_keys, wide, wide_runs, 15)

    def clear(c, carry):
        part[c] = zero
        return carry

    lax.fori_loop(0, 16, clear, 0)
    lax.fori_loop(0, 2, far_to_small, 0)
    for r, q in ((6, 7), (10, 8), (8, 6)):
        arrive(xs.at[r], g_recv.at[q])
        cross(r)
    lax.fori_loop(2, 5, far_to_small, 0)
    arrive(xs.at[pl.ds(1, 8)], cross_recv)
    lax.fori_loop(1, 16, split_block, 0, unroll=5)

    for t in range(16):
        tight[t] = product(t, 0, rp[1, t])
        if t > 0:
            tight[t + 15] = product(t, 1, rp[0, t])
    run_sums(tight_keys, tight, tight_runs, 31)

    def finish_small(c, carry):
        part[c] += wide_runs[wide_last[c]] + tight_runs[tight_last[c]]
        return carry

    lax.fori_loop(0, 16, finish_small, 0)
    part[16] = wide_runs[wide_last[16]] + tight_runs[tight_last[16]]

    for i in (3, 4, 2, 5, 1, 6, 0, 7):
        go(4, 2, part.at[2 * i + 1], cross_in.at[i], back_recv.at[i], partner)

    def fold_rows(value):
        total = value[0:8]
        for q in range(1, B // 8):
            total = total + value[8 * q : 8 * q + 8]
        return total

    def add_inner(c, carry):
        return carry + fold_rows(xs[c] * part[c])

    inner = lax.fori_loop(0, 17, add_inner, jnp.zeros((8, B), F32))
    far_to_large(2)

    def merge(c):
        i = c // 2 - 1 + par
        arrive(cross_in.at[i], back_recv.at[i])
        part[c] += cross_in[i]

    def send_relay(c, h, device, q):
        go(5, 1, part.at[c, half[h]], relay_in.at[3 * h + q], relay_recv.at[h], device)

    def send_near(c, h, q):
        go(5, 1, part.at[c, half[h]], near_in.at[2 * q + h], end_recv.at[0], near(c))

    for c in (8, 6, 10):
        merge(c)
    for h in (0, 1):
        send_relay(8, h, near(4), 0)
        send_relay(10, h, near(-2), 2)
        send_relay(6, h, near(2), 1)
    for c in (2, 14, 4, 12):
        merge(c)
    last = 16 - 16 * par
    i = 7 - 7 * par
    arrive(cross_in.at[i], back_recv.at[i])
    part[last] += cross_in[i]
    for c, q in ((14, 1), (2, 0)):
        for h in (0, 1):
            send_near(c, h, q)
    lax.fori_loop(1, 4, far_pair, 0)

    for e in (1, 3, 2):
        for d in (2, 1, 3):
            q = 3 * (e - 1) + d - 1
            go(6, 1, part.at[slot(e, d, 0, 0), low_half], half_a.at[q], half_recv.at[e - 1], at_y(d))
            go(6, 1, part.at[slot(d, e, 0, 0), high_half], half_b.at[q], half_recv.at[e + 2], at_x(d))

    inner = lax.fori_loop(17, NC, add_inner, inner)
    own = x_ref[...]
    norm = jnp.sum(fold_rows(own * own), axis=0, keepdims=True)
    inner = jnp.sum(inner, axis=0, keepdims=True)
    row_ids = lax.broadcasted_iota(jnp.int32, (8, B), 0)
    v_out[...] = jnp.where(row_ids == 0, inner, jnp.where(row_ids == 1, norm, 0.0))
    for k in range(1, 16):
        remote(v_out, v_near.at[k - 1], sent.at[8], sum_recv.at[0], near(k)).start()

    def send_axis(c, h, q, device):
        go(7, 1, part.at[c, half[h]], axis_in.at[q], end_recv.at[1], device)

    for e in (1, 3, 2):
        send_axis(slot(e, 0, 0, 0), 1, 5 + e, at_x(e))
        send_axis(slot(0, e, 0, 0), 0, 8 + e, at_y(e))

    for h in (0, 1):
        arrive(relay_in.at[pl.ds(3 * h, 3)], relay_recv.at[h])
        part[4, half[h]] += relay_in[3 * h] + relay_in[3 * h + 1]
        part[12, half[h]] += relay_in[3 * h + 2]
        send_near(4, h, 2)
        send_near(12, h, 3)

    arrive(v_near, sum_recv.at[0])
    mid = v_out[...]
    for k in range(15):
        mid = mid + v_near[k]
    v_mid[...] = mid
    for k in range(1, 16):
        remote(v_mid, v_far.at[k - 1], sent.at[9], sum_recv.at[1], near(16 * k)).start()

    for e in (1, 3, 2):
        at = slot(e, 0, 0, 0)
        q = 3 * (e - 1)
        arrive(half_a.at[pl.ds(q, 3)], half_recv.at[e - 1])
        part[at, low_half] += half_a[q] + half_a[q + 1] + half_a[q + 2]
        send_axis(at, 0, e - 1, at_x(e))
        at = slot(0, e, 0, 0)
        arrive(half_b.at[pl.ds(q, 3)], half_recv.at[e + 2])
        part[at, high_half] += half_b[q] + half_b[q + 1] + half_b[q + 2]
        send_axis(at, 1, 2 + e, at_y(e))

    arrive(near_in, end_recv.at[0])
    arrive(axis_in, end_recv.at[1])
    low = part[0, 0:HALF]
    high = part[0, HALF:B]
    for q in range(4):
        low = low + near_in[2 * q]
        high = high + near_in[2 * q + 1]
    for q in range(3):
        low = low + axis_in[q] + axis_in[9 + q]
        high = high + axis_in[3 + q] + axis_in[6 + q]
    image_ref[0:HALF] = low
    image_ref[HALF:B] = high
    arrive(v_far, sum_recv.at[1])
    total = v_mid[...]
    for k in range(15):
        total = total + v_far[k]
    step_ref[...] = jnp.broadcast_to(total[1:2] / total[0:1], (8, B))
    for group, count in enumerate(halves_sent):
        whole = tf.at[pl.ds(0, count // 2)]
        remote(whole, whole, sent.at[group], block_recv, partner).wait_send()
    remote(v_near, v_near, sent.at[8], block_recv, partner).wait_send()
    remote(v_near, v_near, sent.at[9], block_recv, partner).wait_send()


def update_kernel(x_ref, image_ref, step_ref, sol_ref, res_ref):
    own = x_ref[...]
    step = step_ref[0:1]
    sol_ref[...] = step * own
    res_ref[...] = own - step * image_ref[...]


def per_device(right_side, kernel_tiles, route_pairs):
    vmem = pltpu.VMEM
    dma = pltpu.SemaphoreType.DMA
    sems = [dma((10,)), dma((9,)), dma((6,)), dma(()), dma(()), dma((8,)), dma((2,)), dma((6,)), dma((2,)), dma((2,))]
    block = jax.ShapeDtypeStruct((B, B), F32)
    whole = pl.BlockSpec(memory_space=vmem)
    image, step = pl.pallas_call(
        cg_kernel,
        out_shape=(block, jax.ShapeDtypeStruct((8, B), F32)),
        in_specs=[pl.BlockSpec(memory_space=pltpu.SMEM), whole, pl.BlockSpec(memory_space=pl.ANY)],
        out_specs=(whole, whole),
        scratch_shapes=[
            vmem((NT, B, B), F32),
            vmem((NT, 2, B, 2 * B), BF16),
            vmem((NC, B, B), F32),
            vmem((NC, 2 * B, 2 * B), BF16),
            vmem((NC, B, B), F32),
            vmem((16, B, B), F32),
            vmem((31, B, B), F32),
            vmem((16, B, B), F32),
            vmem((32, B, B), F32),
            vmem((8, B, B), F32),
            vmem((6, HALF, B), F32),
            vmem((8, HALF, B), F32),
            vmem((12, HALF, B), F32),
            vmem((9, HALF, B), F32),
            vmem((9, HALF, B), F32),
            vmem((8, B), F32),
            vmem((8, B), F32),
            vmem((15, 8, B), F32),
            vmem((15, 8, B), F32),
            pltpu.SMEM((16,), jnp.int32),
            pltpu.SMEM((32,), jnp.int32),
            pltpu.SMEM((NC,), jnp.int32),
            pltpu.SMEM((NC,), jnp.int32),
            dma((CHUNKS,)),
        ]
        + sems,
        compiler_params=pltpu.CompilerParams(
            collective_id=0, has_side_effects=True, vmem_limit_bytes=60 * 1024 * 1024
        ),
    )(route_pairs.T, right_side, kernel_tiles)
    return pl.pallas_call(
        update_kernel,
        out_shape=(block, block),
        in_specs=[whole, whole, whole],
        out_specs=(whole, whole),
    )(right_side, image, step)


def solution(mesh):
    return jax.shard_map(
        per_device,
        mesh=mesh,
        in_specs=(P("blk", None), P("blk", None, None, None), P()),
        out_specs=(P("blk", None), P("blk", None)),
        check_vma=False,
    )
```

```python
import functools

import jax
import jax.numpy as jnp
from jax import lax
from jax.experimental import pallas as pl
from jax.experimental.pallas import tpu as pltpu
from jax.sharding import PartitionSpec as P

MESH = pl.DeviceIdType.MESH
NB = 256
B = 128
NT = 129
NC = 31
CHUNK = 16
CHUNKS = 9
HALF = B // 2
X_FIRST = 64
F32 = jnp.float32
BF16 = jnp.bfloat16


def split_pair(value):
    high = value.astype(BF16)
    low = (value - high.astype(F32)).astype(BF16)
    return high, low


def sort_network(count):
    pairs = []
    p = 1
    while p < count:
        k = p
        while k >= 1:
            for j in range(k % p, count - k, 2 * k):
                for i in range(min(k, count - j - k)):
                    if (i + j) // (2 * p) == (i + j + k) // (2 * p):
                        pairs.append((i + j, i + j + k))
            k //= 2
        p *= 2
    return pairs


def cg_kernel(
    rp, x_ref, tiles, image_ref, step_ref,
    tf, tb, xs, wb, part, wide, tight, wide_runs, tight_runs,
    cross_in, relay_in, near_in, axis_low, axis_high, half_a, half_b,
    v_out, v_mid, v_near, v_far, wide_keys, tight_keys, wide_last, tight_last,
    tile_sem, sent, g_recv, first_recv, early_recv, block_recv, cross_recv, back_recv, relay_recv, half_recv, end_recv, sum_recv,
):
    me = lax.axis_index("blk")
    par = lax.rem(me, 2)
    partner = me + 1 - 2 * par
    col = me // 16
    px = me // 64
    py = lax.rem(col, 4)

    def near(step):
        return lax.rem(me + step + NB, NB)

    def at_x(step):
        return me + (lax.rem(px + step, 4) - px) * 64

    def at_y(step):
        return me + (lax.rem(py + step, 4) - py) * 16

    def slot(dx, dy, tx, ty):
        owner_col = lax.rem(px + dx, 4) * 4 + lax.rem(py + dy, 4)
        there_col = lax.rem(px + tx, 4) * 4 + lax.rem(py + ty, 4)
        return 15 + lax.rem(owner_col - there_col + 16, 16)

    def remote(src, dst, send_sem, recv_sem, device):
        return pltpu.make_async_remote_copy(
            src_ref=src, dst_ref=dst, send_sem=send_sem, recv_sem=recv_sem,
            device_id=(device,), device_id_type=MESH,
        )

    def arrive(dst, recv_sem):
        remote(dst, dst, sent.at[0], recv_sem, partner).wait_recv()

    half = [pl.ds(0, HALF), pl.ds(HALF, HALF)]
    x_rows, y_rows = pl.ds(0, X_FIRST), pl.ds(X_FIRST, B - X_FIRST)
    rows_sent = [0] * 8

    def go(group, rows, src, dst, recv_sem, device):
        rows_sent[group] += rows
        remote(src, dst, sent.at[group], recv_sem, device).start()

    def tile_copy(q, count):
        span = pl.ds(q * CHUNK, count)
        return pltpu.make_async_copy(tiles.at[0, span], tf.at[span], tile_sem.at[q])


    barrier = pltpu.get_barrier_semaphore()
    axis_devices = [at_x(d) for d in (1, 2, 3)] + [at_y(d) for d in (1, 2, 3)]
    for device in axis_devices + [near(2), near(4), near(12), near(14), near(-2), near(-4), partner]:
        pl.semaphore_signal(barrier, inc=1, device_id=(device,), device_id_type=MESH)
    pl.semaphore_wait(barrier, 13)

    def own_to_x(d, rows, sem):
        go(0, rows.size, x_ref.at[rows], xs.at[slot(0, 0, d, 0), rows], sem, at_x(d))

    def own_to_y(d, rows, sem):
        go(0, rows.size, x_ref.at[rows], xs.at[slot(0, 0, 0, d), rows], sem, at_y(d))

    for h in (0, 1):
        go(1, HALF, x_ref.at[half[1 - h]], xs.at[12, half[1 - h]], g_recv.at[3 - h], near(-12))
        go(1, HALF, x_ref.at[half[h]], xs.at[4, half[h]], g_recv.at[h], near(-4))
    for d in (2, 1, 3):
        own_to_x(d, x_rows, first_recv.at[d - 1])
        own_to_y(d, y_rows, first_recv.at[2 + d])
    go(1, B, x_ref, xs.at[2], g_recv.at[4], near(-2))
    go(1, B, x_ref, xs.at[14], g_recv.at[5], near(-14))
    xs[0] = x_ref[...]
    for q in range(CHUNKS - 1):
        tile_copy(q, CHUNK).start()
    tile_copy(CHUNKS - 1, 1).start()

    def ordered(keys, count):
        keys = list(keys)
        for lower, upper in sort_network(count):
            if upper < len(keys):
                small, big = jnp.minimum(keys[lower], keys[upper]), jnp.maximum(keys[lower], keys[upper])
                keys[lower], keys[upper] = small, big
        return keys

    keys = [rp[0, 16 * m] * 32 + m - 1 for m in range(1, 9)]
    keys += [rp[1, 16 * m] * 32 + m + 7 for m in range(1, 8)]
    for i, key in enumerate(ordered(keys, 16)):
        wide_keys[i] = key
    keys = [rp[0, t] * 32 + t for t in range(16)] + [rp[1, t] * 32 + t + 15 for t in range(1, 16)]
    for i, key in enumerate(ordered(keys, 32)):
        tight_keys[i] = key

    def find_last(c, carry):
        for keys, last, count in ((wide_keys, wide_last, 15), (tight_keys, tight_last, 31)):
            found = jnp.int32(-1)
            for i in range(count):
                found = found + (keys[i] < (c + 1) * 32).astype(jnp.int32)
            ends_here = lax.div(keys[jnp.maximum(found, 0)], 32) == c
            last[c] = jnp.where(ends_here, found, count)
        return carry

    lax.fori_loop(0, NC, find_last, 0)


    def split_tile(t):
        high, low = split_pair(tf[t])
        tb[t, 0, :, 0:B] = high
        tb[t, 0, :, B : 2 * B] = low
        tb[t, 1, :, 0:B] = high.T
        tb[t, 1, :, B : 2 * B] = low.T

    def prepare(q, carry):
        tile_copy(q, CHUNK).wait()
        for u in range(CHUNK):
            split_tile(q * CHUNK + u)
        return carry

    def cross(r):
        go(2, B, xs.at[r], xs.at[r - 1 + 2 * par], cross_recv, partner)

    def forward(e):
        src = slot(e, 0, 0, 0)
        arrive(xs.at[src, x_rows], first_recv.at[3 - e])
        for d in (2, 1, 3):
            sem = early_recv if (e, d) == (1, 3) else block_recv
            go(3, X_FIRST, xs.at[src, x_rows], xs.at[slot(e, 0, 0, d), x_rows], sem, at_y(d))
        src = slot(0, e, 0, 0)
        arrive(xs.at[src, y_rows], first_recv.at[6 - e])
        for d in (2, 1, 3):
            sem = early_recv if (e, d) == (1, 3) else block_recv
            go(3, B - X_FIRST, xs.at[src, y_rows], xs.at[slot(0, e, d, 0), y_rows], sem, at_x(d))

    def forward_4(h):
        arrive(xs.at[4, half[h]], g_recv.at[h])
        if h == 0:
            go(1, HALF, xs.at[4, half[0]], xs.at[8, half[0]], g_recv.at[6], near(-4))
        go(1, HALF, xs.at[4, half[h]], xs.at[6, half[h]], g_recv.at[7], near(-2))

    def forward_12(h):
        arrive(xs.at[12, half[h]], g_recv.at[2 + h])
        if h == 1:
            go(1, HALF, xs.at[12, half[1]], xs.at[8, half[1]], g_recv.at[9], near(4))
        go(1, HALF, xs.at[12, half[h]], xs.at[10, half[h]], g_recv.at[8], near(2))

    forward(3)
    forward_4(0)
    forward(1)
    forward_4(1)
    forward_12(1)
    forward_12(0)
    for d in (3, 1, 2):
        own_to_y(d, x_rows, early_recv if d == 3 else block_recv)
        own_to_x(d, y_rows, block_recv)
    lax.fori_loop(0, 3, prepare, 0)
    forward(2)
    lax.fori_loop(3, CHUNKS - 1, prepare, 0)
    tile_copy(CHUNKS - 1, 1).wait()
    split_tile(NT - 1)
    for r in (4, 12):
        cross(r)
    for r, q in ((2, 4), (14, 5)):
        arrive(xs.at[r], g_recv.at[q])
        cross(r)

    def split_block(c, carry):
        high, low = split_pair(xs[c])
        wb[c, 0:B, 0:B] = high
        wb[c, 0:B, B : 2 * B] = low
        wb[c, B : 2 * B, 0:B] = high
        wb[c, B : 2 * B, B : 2 * B] = low
        return carry

    def product(t, turn, c):
        both = jnp.dot(tb[t, turn], wb[c], preferred_element_type=F32)
        return both[:, 0:B] + both[:, B : 2 * B]

    def as_mask(flag):
        return flag.astype(jnp.int32).astype(F32)

    zero = jnp.zeros((B, B), F32)

    def run_sums(keys, products, runs, count):
        total = zero
        for i in range(count):
            key = keys[i]
            before = keys[max(i - 1, 0)]
            total = as_mask(lax.div(before, 32) == lax.div(key, 32)) * total + products[lax.rem(key, 32)]
            runs[i] = total
        runs[count] = zero

    def orient(t, j, k):
        ahead = rp[0, t] == j
        small = jnp.where(ahead, j, 16 - j)
        large = jnp.where(ahead, 15 + k, 32 - k)
        return jnp.where(ahead, 0, 1), small, large, as_mask(ahead)

    def one_to_small(j):
        first, second = zero, zero
        for k in range(2, 9):
            turn, _, large, mask = orient(16 * k - j, j, k)
            value = product(16 * k - j, turn, large)
            first = first + mask * value
            second = second + (1.0 - mask) * value
        return first, second

    def far_to_small(j):
        first, second = one_to_small(j)
        third, fourth = one_to_small(16 - j)
        part[j] = first + fourth
        part[16 - j] = second + third

    def small_pair(i, carry):
        far_to_small(2 * i + 1)
        far_to_small(2 * i + 2)
        return carry

    def far_to_large(k):
        first, second = zero, zero
        for j in range(1, 16):
            turn, small, _, mask = orient(16 * k - j, j, k)
            value = product(16 * k - j, 1 - turn, small)
            first = first + mask * value
            second = second + (1.0 - mask) * value
        part[15 + k] = first
        part[32 - k] = second

    def large_pair(i, carry):
        far_to_large(2 * i + 1)
        far_to_large(2 * i + 2)
        return carry

    def add_runs(c, carry):
        part[c] += wide_runs[wide_last[c]] + tight_runs[tight_last[c]]
        return carry

    arrive(xs.at[pl.ds(0, 12), pl.ds(0, 16)], early_recv)
    go(2, B, xs.at[16 - 16 * par], xs.at[15 - 14 * par], cross_recv, partner)
    arrive(xs.at[pl.ds(0, 21), y_rows], block_recv)
    split_block(0, 0)
    lax.fori_loop(16, NC, split_block, 0, unroll=5)
    for m in range(1, 9):
        wide[m - 1] = product(16 * m, 0, rp[1, 16 * m])
        if m < 8:
            wide[m + 7] = product(16 * m, 1, rp[0, 16 * m])
    run_sums(wide_keys, wide, wide_runs, 15)
    for r, q in ((6, 7), (10, 8)):
        arrive(xs.at[r], g_recv.at[q])
        cross(r)
    lax.fori_loop(0, 2, small_pair, 0)
    arrive(xs.at[8, half[0]], g_recv.at[6])
    arrive(xs.at[8, half[1]], g_recv.at[9])
    cross(8)
    lax.fori_loop(2, 3, small_pair, 0)
    far_to_small(7)
    first, second = one_to_small(8)
    part[8] = first + second

    arrive(xs.at[pl.ds(1, 8)], cross_recv)
    lax.fori_loop(1, 16, split_block, 0, unroll=5)
    for t in range(16):
        tight[t] = product(t, 0, rp[1, t])
        if t > 0:
            tight[t + 15] = product(t, 1, rp[0, t])
    run_sums(tight_keys, tight, tight_runs, 31)

    def cross_back(i):
        go(4, B, part.at[2 * i + 1], cross_in.at[i], back_recv.at[i], partner)

    def finish_small(c, carry):
        part[c] += tight_runs[tight_last[c]]
        return carry

    lax.fori_loop(1, 16, finish_small, 0, unroll=5)
    for i in (3, 4, 2, 5, 1, 6, 0, 7):
        cross_back(i)
    part[0] = wide_runs[wide_last[0]] + tight_runs[tight_last[0]]
    part[16] = wide_runs[wide_last[16]] + tight_runs[tight_last[16]]

    def fold_rows(value):
        total = value[0:8]
        for q in range(1, B // 8):
            total = total + value[8 * q : 8 * q + 8]
        return total

    def add_inner(c, carry):
        return carry + fold_rows(xs[c] * part[c])

    inner = lax.fori_loop(0, 17, add_inner, jnp.zeros((8, B), F32), unroll=6)

    def merge(c):
        i = c // 2 - 1 + par
        arrive(cross_in.at[i], back_recv.at[i])
        part[c] += cross_in[i]

    def send_near(c, h, q):
        go(5, HALF, part.at[c, half[h]], near_in.at[2 * q + h], end_recv.at[0], near(c))

    far_to_large(2)
    for c in (8, 6, 10):
        merge(c)
    def send_relay(c, h, q, device):
        go(5, HALF, part.at[c, half[h]], relay_in.at[q], relay_recv.at[q // 3], device)

    send_relay(8, 0, 2, near(4))
    send_relay(8, 1, 5, near(-4))
    for h in (0, 1):
        send_relay(6, h, h, near(2))
        send_relay(10, h, 3 + h, near(-2))
    lax.fori_loop(1, 4, large_pair, 0)
    lax.fori_loop(17, NC, add_runs, 0, unroll=7)
    inner = lax.fori_loop(17, NC, add_inner, inner, unroll=7)
    own = x_ref[...]
    norm = jnp.sum(fold_rows(own * own), axis=0, keepdims=True)
    inner = jnp.sum(inner, axis=0, keepdims=True)
    row_ids = lax.broadcasted_iota(jnp.int32, (8, B), 0)
    v_out[...] = jnp.where(row_ids == 0, inner, jnp.where(row_ids == 1, norm, 0.0))
    for k in range(15, 0, -1):
        remote(v_out, v_near.at[k - 1], sent.at[8], sum_recv.at[0], near(k)).start()
    last = 16 - 16 * par
    i = 7 - 7 * par
    arrive(cross_in.at[i], back_recv.at[i])
    part[last] += cross_in[i]
    for e in (1, 3, 2):
        for d in (2, 1, 3):
            q = 3 * (e - 1) + d - 1
            go(6, X_FIRST, part.at[slot(e, d, 0, 0), x_rows], half_a.at[q], half_recv.at[e - 1], at_y(d))
            go(6, B - X_FIRST, part.at[slot(d, e, 0, 0), y_rows], half_b.at[q], half_recv.at[e + 2], at_x(d))
    for c in (14, 2, 12, 4):
        merge(c)
    for c, q in ((14, 1), (2, 0)):
        for h in (0, 1):
            send_near(c, h, q)

    def send_axis(c, rows, dst, device):
        go(7, rows.size, part.at[c, rows], dst, end_recv.at[1], device)

    for e in (1, 3, 2):
        send_axis(slot(e, 0, 0, 0), y_rows, axis_high.at[2 + e], at_x(e))
        send_axis(slot(0, e, 0, 0), x_rows, axis_low.at[2 + e], at_y(e))

    arrive(relay_in.at[pl.ds(0, 3)], relay_recv.at[0])
    part[4, half[0]] += relay_in[0] + relay_in[2]
    part[4, half[1]] += relay_in[1]
    for h in (0, 1):
        send_near(4, h, 2)
    arrive(relay_in.at[pl.ds(3, 3)], relay_recv.at[1])
    part[12, half[0]] += relay_in[3]
    part[12, half[1]] += relay_in[4] + relay_in[5]
    for h in (0, 1):
        send_near(12, h, 3)

    arrive(v_near, sum_recv.at[0])
    mid = v_out[...]
    for k in range(15):
        mid = mid + v_near[k]
    v_mid[...] = mid
    for k in range(1, 16):
        remote(v_mid, v_far.at[k - 1], sent.at[9], sum_recv.at[1], near(16 * k)).start()

    for e in (1, 3, 2):
        at = slot(e, 0, 0, 0)
        q = 3 * (e - 1)
        arrive(half_a.at[pl.ds(q, 3)], half_recv.at[e - 1])
        part[at, x_rows] += half_a[q] + half_a[q + 1] + half_a[q + 2]
        send_axis(at, x_rows, axis_low.at[e - 1], at_x(e))
        at = slot(0, e, 0, 0)
        arrive(half_b.at[pl.ds(q, 3)], half_recv.at[e + 2])
        part[at, y_rows] += half_b[q] + half_b[q + 1] + half_b[q + 2]
        send_axis(at, y_rows, axis_high.at[e - 1], at_y(e))

    arrive(near_in, end_recv.at[0])
    arrive(xs.at[pl.ds(0, 6)], end_recv.at[1])
    low = part[0, 0:HALF]
    high = part[0, HALF:B]
    for q in range(4):
        low = low + near_in[2 * q]
        high = high + near_in[2 * q + 1]
    image_ref[0:HALF] = low
    image_ref[HALF:B] = high
    low = image_ref[0:X_FIRST]
    high = image_ref[X_FIRST:B]
    for q in range(6):
        low = low + axis_low[q]
        high = high + axis_high[q]
    image_ref[0:X_FIRST] = low
    image_ref[X_FIRST:B] = high
    arrive(v_far, sum_recv.at[1])
    total = v_mid[...]
    for k in range(15):
        total = total + v_far[k]
    step_ref[...] = jnp.broadcast_to(total[1:2] / total[0:1], (8, B))
    for group, rows in enumerate(rows_sent):
        whole = tf.at[pl.ds(0, rows // B)]
        remote(whole, whole, sent.at[group], block_recv, partner).wait_send()
    remote(v_near, v_near, sent.at[8], block_recv, partner).wait_send()
    remote(v_near, v_near, sent.at[9], block_recv, partner).wait_send()


def update_kernel(x_ref, image_ref, step_ref, sol_ref, res_ref):
    own = x_ref[...]
    step = step_ref[0:1]
    sol_ref[...] = step * own
    res_ref[...] = own - step * image_ref[...]


def per_device(right_side, kernel_tiles, route_pairs):
    vmem = pltpu.VMEM
    dma = pltpu.SemaphoreType.DMA
    sems = [dma((10,)), dma((10,)), dma((6,)), dma(()), dma(()), dma(()), dma((8,)), dma((2,)), dma((6,)), dma((2,)), dma((2,))]
    block = jax.ShapeDtypeStruct((B, B), F32)
    whole = pl.BlockSpec(memory_space=vmem)
    image, step = pl.pallas_call(
        cg_kernel,
        out_shape=(block, jax.ShapeDtypeStruct((8, B), F32)),
        in_specs=[pl.BlockSpec(memory_space=pltpu.SMEM), whole, pl.BlockSpec(memory_space=pl.ANY)],
        out_specs=(whole, whole),
        scratch_shapes=[
            vmem((NT, B, B), F32),
            vmem((NT, 2, B, 2 * B), BF16),
            vmem((NC, B, B), F32),
            vmem((NC, 2 * B, 2 * B), BF16),
            vmem((NC, B, B), F32),
            vmem((16, B, B), F32),
            vmem((31, B, B), F32),
            vmem((16, B, B), F32),
            vmem((32, B, B), F32),
            vmem((8, B, B), F32),
            vmem((6, HALF, B), F32),
            vmem((8, HALF, B), F32),
            vmem((6, X_FIRST, B), F32),
            vmem((6, B - X_FIRST, B), F32),
            vmem((9, X_FIRST, B), F32),
            vmem((9, B - X_FIRST, B), F32),
            vmem((8, B), F32),
            vmem((8, B), F32),
            vmem((15, 8, B), F32),
            vmem((15, 8, B), F32),
            pltpu.SMEM((16,), jnp.int32),
            pltpu.SMEM((32,), jnp.int32),
            pltpu.SMEM((NC,), jnp.int32),
            pltpu.SMEM((NC,), jnp.int32),
            dma((CHUNKS,)),
        ]
        + sems,
        compiler_params=pltpu.CompilerParams(
            collective_id=0, has_side_effects=True, vmem_limit_bytes=60 * 1024 * 1024
        ),
    )(route_pairs.T, right_side, kernel_tiles)
    return pl.pallas_call(
        update_kernel,
        out_shape=(block, block),
        in_specs=[whole, whole, whole],
        out_specs=(whole, whole),
    )(right_side, image, step)


def solution(mesh):
    return jax.shard_map(
        per_device,
        mesh=mesh,
        in_specs=(P("blk", None), P("blk", None, None, None), P()),
        out_specs=(P("blk", None), P("blk", None)),
        check_vma=False,
    )
```

```python
import functools

import jax
import jax.numpy as jnp
from jax import lax
from jax.experimental import pallas as pl
from jax.experimental.pallas import tpu as pltpu
from jax.sharding import PartitionSpec as P

MESH = pl.DeviceIdType.MESH
NB = 256
B = 128
NT = 129
NC = 31
CHUNK = 16
CHUNKS = 9
HALF = B // 2
X_FIRST = 64
F32 = jnp.float32
BF16 = jnp.bfloat16


def split_pair(value):
    high = value.astype(BF16)
    low = (value - high.astype(F32)).astype(BF16)
    return high, low


def sort_network(count):
    pairs = []
    p = 1
    while p < count:
        k = p
        while k >= 1:
            for j in range(k % p, count - k, 2 * k):
                for i in range(min(k, count - j - k)):
                    if (i + j) // (2 * p) == (i + j + k) // (2 * p):
                        pairs.append((i + j, i + j + k))
            k //= 2
        p *= 2
    return pairs


def cg_kernel(
    pairs_hbm, x_hbm, tiles, image_ref, step_ref,
    rp,
    tf, tb, xs, wb, part, wide, tight, wide_runs, tight_runs,
    cross_in, relay_in, near_in, axis_low, axis_high, half_a, half_b,
    v_out, v_mid, v_near, v_far, wide_keys, tight_keys, wide_last, tight_last,
    tile_sem, own_sem, pairs_sem, sent, g_recv, first_recv, early_recv, block_recv, cross_recv, back_recv, relay_recv, half_recv, end_recv, sum_recv,
):
    me = lax.axis_index("blk")
    par = lax.rem(me, 2)
    partner = me + 1 - 2 * par
    col = me // 16
    px = me // 64
    py = lax.rem(col, 4)

    def near(step):
        return lax.rem(me + step + NB, NB)

    def at_x(step):
        return me + (lax.rem(px + step, 4) - px) * 64

    def at_y(step):
        return me + (lax.rem(py + step, 4) - py) * 16

    def slot(dx, dy, tx, ty):
        owner_col = lax.rem(px + dx, 4) * 4 + lax.rem(py + dy, 4)
        there_col = lax.rem(px + tx, 4) * 4 + lax.rem(py + ty, 4)
        return 15 + lax.rem(owner_col - there_col + 16, 16)

    def remote(src, dst, send_sem, recv_sem, device):
        return pltpu.make_async_remote_copy(
            src_ref=src, dst_ref=dst, send_sem=send_sem, recv_sem=recv_sem,
            device_id=(device,), device_id_type=MESH,
        )

    def arrive(dst, recv_sem):
        remote(dst, dst, sent.at[0], recv_sem, partner).wait_recv()

    half = [pl.ds(0, HALF), pl.ds(HALF, HALF)]
    x_rows, y_rows = pl.ds(0, X_FIRST), pl.ds(X_FIRST, B - X_FIRST)
    rows_sent = [0] * 8

    def go(group, rows, src, dst, recv_sem, device):
        rows_sent[group] += rows
        remote(src, dst, sent.at[group], recv_sem, device).start()

    own_copy = pltpu.make_async_copy(x_hbm, xs.at[0], own_sem)
    own_copy.start()
    pairs_copy = pltpu.make_async_copy(pairs_hbm, rp, pairs_sem)
    pairs_copy.start()

    def tile_copy(q, count):
        span = pl.ds(q * CHUNK, count)
        return pltpu.make_async_copy(tiles.at[0, span], tf.at[span], tile_sem.at[q])


    barrier = pltpu.get_barrier_semaphore()
    axis_devices = [at_x(d) for d in (1, 2, 3)] + [at_y(d) for d in (1, 2, 3)]
    for device in axis_devices + [near(2), near(4), near(12), near(14), near(-2), near(-4), partner]:
        pl.semaphore_signal(barrier, inc=1, device_id=(device,), device_id_type=MESH)
    own_copy.wait()
    pl.semaphore_wait(barrier, 13)

    def own_to_x(d, rows, sem):
        go(0, rows.size, xs.at[0, rows], xs.at[slot(0, 0, d, 0), rows], sem, at_x(d))

    def own_to_y(d, rows, sem):
        go(0, rows.size, xs.at[0, rows], xs.at[slot(0, 0, 0, d), rows], sem, at_y(d))

    for h in (0, 1):
        go(1, HALF, xs.at[0, half[1 - h]], xs.at[12, half[1 - h]], g_recv.at[3 - h], near(-12))
        go(1, HALF, xs.at[0, half[h]], xs.at[4, half[h]], g_recv.at[h], near(-4))
    for d in (2, 1, 3):
        own_to_x(d, x_rows, first_recv.at[d - 1])
        own_to_y(d, y_rows, first_recv.at[2 + d])
    go(1, B, xs.at[0], xs.at[2], g_recv.at[4], near(-2))
    go(1, B, xs.at[0], xs.at[14], g_recv.at[5], near(-14))
    for q in range(CHUNKS - 1):
        tile_copy(q, CHUNK).start()
    tile_copy(CHUNKS - 1, 1).start()

    def ordered(keys, count):
        keys = list(keys)
        for lower, upper in sort_network(count):
            if upper < len(keys):
                small, big = jnp.minimum(keys[lower], keys[upper]), jnp.maximum(keys[lower], keys[upper])
                keys[lower], keys[upper] = small, big
        return keys

    pairs_copy.wait()
    keys = [rp[0, 16 * m] * 32 + m - 1 for m in range(1, 9)]
    keys += [rp[1, 16 * m] * 32 + m + 7 for m in range(1, 8)]
    for i, key in enumerate(ordered(keys, 16)):
        wide_keys[i] = key
    keys = [rp[0, t] * 32 + t for t in range(16)] + [rp[1, t] * 32 + t + 15 for t in range(1, 16)]
    for i, key in enumerate(ordered(keys, 32)):
        tight_keys[i] = key

    def find_last(c, carry):
        for keys, last, count in ((wide_keys, wide_last, 15), (tight_keys, tight_last, 31)):
            found = jnp.int32(-1)
            for i in range(count):
                found = found + (keys[i] < (c + 1) * 32).astype(jnp.int32)
            ends_here = lax.div(keys[jnp.maximum(found, 0)], 32) == c
            last[c] = jnp.where(ends_here, found, count)
        return carry

    lax.fori_loop(0, NC, find_last, 0)


    def split_tile(t):
        high, low = split_pair(tf[t])
        tb[t, 0, :, 0:B] = high
        tb[t, 0, :, B : 2 * B] = low
        tb[t, 1, :, 0:B] = high.T
        tb[t, 1, :, B : 2 * B] = low.T

    def prepare(q, carry):
        tile_copy(q, CHUNK).wait()
        for u in range(CHUNK):
            split_tile(q * CHUNK + u)
        return carry

    def cross(r):
        go(2, B, xs.at[r], xs.at[r - 1 + 2 * par], cross_recv, partner)

    def forward(e):
        src = slot(e, 0, 0, 0)
        arrive(xs.at[src, x_rows], first_recv.at[3 - e])
        for d in (2, 1, 3):
            sem = early_recv if (e, d) == (1, 3) else block_recv
            go(3, X_FIRST, xs.at[src, x_rows], xs.at[slot(e, 0, 0, d), x_rows], sem, at_y(d))
        src = slot(0, e, 0, 0)
        arrive(xs.at[src, y_rows], first_recv.at[6 - e])
        for d in (2, 1, 3):
            sem = early_recv if (e, d) == (1, 3) else block_recv
            go(3, B - X_FIRST, xs.at[src, y_rows], xs.at[slot(0, e, d, 0), y_rows], sem, at_x(d))

    def forward_4(h):
        arrive(xs.at[4, half[h]], g_recv.at[h])
        if h == 0:
            go(1, HALF, xs.at[4, half[0]], xs.at[8, half[0]], g_recv.at[6], near(-4))
        go(1, HALF, xs.at[4, half[h]], xs.at[6, half[h]], g_recv.at[7], near(-2))

    def forward_12(h):
        arrive(xs.at[12, half[h]], g_recv.at[2 + h])
        if h == 1:
            go(1, HALF, xs.at[12, half[1]], xs.at[8, half[1]], g_recv.at[9], near(4))
        go(1, HALF, xs.at[12, half[h]], xs.at[10, half[h]], g_recv.at[8], near(2))

    forward(3)
    forward_4(0)
    forward(1)
    forward_4(1)
    forward_12(1)
    forward_12(0)
    for d in (3, 1, 2):
        own_to_y(d, x_rows, early_recv if d == 3 else block_recv)
        own_to_x(d, y_rows, block_recv)
    lax.fori_loop(0, 3, prepare, 0)
    forward(2)
    lax.fori_loop(3, CHUNKS - 1, prepare, 0)
    tile_copy(CHUNKS - 1, 1).wait()
    split_tile(NT - 1)
    for r in (4, 12):
        cross(r)
    for r, q in ((2, 4), (14, 5)):
        arrive(xs.at[r], g_recv.at[q])
        cross(r)

    def split_block(c, carry):
        high, low = split_pair(xs[c])
        wb[c, 0:B, 0:B] = high
        wb[c, 0:B, B : 2 * B] = low
        wb[c, B : 2 * B, 0:B] = high
        wb[c, B : 2 * B, B : 2 * B] = low
        return carry

    def product(t, turn, c):
        both = jnp.dot(tb[t, turn], wb[c], preferred_element_type=F32)
        return both[:, 0:B] + both[:, B : 2 * B]

    def as_mask(flag):
        return flag.astype(jnp.int32).astype(F32)

    zero = jnp.zeros((B, B), F32)

    def run_sums(keys, products, runs, count):
        total = zero
        for i in range(count):
            key = keys[i]
            before = keys[max(i - 1, 0)]
            total = as_mask(lax.div(before, 32) == lax.div(key, 32)) * total + products[lax.rem(key, 32)]
            runs[i] = total
        runs[count] = zero

    def orient(t, j, k):
        ahead = rp[0, t] == j
        small = jnp.where(ahead, j, 16 - j)
        large = jnp.where(ahead, 15 + k, 32 - k)
        return jnp.where(ahead, 0, 1), small, large, as_mask(ahead)

    def one_to_small(j):
        first, second = zero, zero
        for k in range(2, 9):
            turn, _, large, mask = orient(16 * k - j, j, k)
            value = product(16 * k - j, turn, large)
            first = first + mask * value
            second = second + (1.0 - mask) * value
        return first, second

    def far_to_small(j):
        first, second = one_to_small(j)
        third, fourth = one_to_small(16 - j)
        part[j] = first + fourth
        part[16 - j] = second + third

    def small_pair(i, carry):
        far_to_small(2 * i + 1)
        far_to_small(2 * i + 2)
        return carry

    def far_to_large(k):
        first, second = zero, zero
        for j in range(1, 16):
            turn, small, _, mask = orient(16 * k - j, j, k)
            value = product(16 * k - j, 1 - turn, small)
            first = first + mask * value
            second = second + (1.0 - mask) * value
        part[15 + k] = first
        part[32 - k] = second

    def large_pair(i, carry):
        far_to_large(2 * i + 1)
        far_to_large(2 * i + 2)
        return carry

    def add_runs(c, carry):
        part[c] += wide_runs[wide_last[c]] + tight_runs[tight_last[c]]
        return carry

    arrive(xs.at[pl.ds(0, 12), pl.ds(0, 16)], early_recv)
    go(2, B, xs.at[16 - 16 * par], xs.at[15 - 14 * par], cross_recv, partner)
    arrive(xs.at[pl.ds(0, 21), y_rows], block_recv)
    split_block(0, 0)
    lax.fori_loop(16, NC, split_block, 0, unroll=5)
    for m in range(1, 9):
        wide[m - 1] = product(16 * m, 0, rp[1, 16 * m])
        if m < 8:
            wide[m + 7] = product(16 * m, 1, rp[0, 16 * m])
    run_sums(wide_keys, wide, wide_runs, 15)
    for r, q in ((6, 7), (10, 8)):
        arrive(xs.at[r], g_recv.at[q])
        cross(r)
    lax.fori_loop(0, 2, small_pair, 0)
    arrive(xs.at[8, half[0]], g_recv.at[6])
    arrive(xs.at[8, half[1]], g_recv.at[9])
    cross(8)
    lax.fori_loop(2, 3, small_pair, 0)
    far_to_small(7)
    first, second = one_to_small(8)
    part[8] = first + second

    arrive(xs.at[pl.ds(1, 8)], cross_recv)
    lax.fori_loop(1, 16, split_block, 0, unroll=5)
    for t in range(16):
        tight[t] = product(t, 0, rp[1, t])
        if t > 0:
            tight[t + 15] = product(t, 1, rp[0, t])
    run_sums(tight_keys, tight, tight_runs, 31)

    def cross_back(i):
        go(4, B, part.at[2 * i + 1], cross_in.at[i], back_recv.at[i], partner)

    def finish_small(c, carry):
        part[c] += tight_runs[tight_last[c]]
        return carry

    lax.fori_loop(1, 16, finish_small, 0, unroll=5)
    for i in (3, 4, 2, 5, 1, 6, 0, 7):
        cross_back(i)
    part[0] = wide_runs[wide_last[0]] + tight_runs[tight_last[0]]
    part[16] = wide_runs[wide_last[16]] + tight_runs[tight_last[16]]

    def fold_rows(value):
        total = value[0:8]
        for q in range(1, B // 8):
            total = total + value[8 * q : 8 * q + 8]
        return total

    def add_inner(c, carry):
        return carry + fold_rows(xs[c] * part[c])

    inner = lax.fori_loop(0, 17, add_inner, jnp.zeros((8, B), F32), unroll=6)

    def merge(c):
        i = c // 2 - 1 + par
        arrive(cross_in.at[i], back_recv.at[i])
        part[c] += cross_in[i]

    def send_near(c, h, q):
        go(5, HALF, part.at[c, half[h]], near_in.at[2 * q + h], end_recv.at[0], near(c))

    far_to_large(2)
    for c in (8, 6, 10):
        merge(c)
    def send_relay(c, h, q, device):
        go(5, HALF, part.at[c, half[h]], relay_in.at[q], relay_recv.at[q // 3], device)

    send_relay(8, 0, 2, near(4))
    send_relay(8, 1, 5, near(-4))
    for h in (0, 1):
        send_relay(6, h, h, near(2))
        send_relay(10, h, 3 + h, near(-2))
    lax.fori_loop(1, 4, large_pair, 0)
    lax.fori_loop(17, NC, add_runs, 0, unroll=7)
    inner = lax.fori_loop(17, NC, add_inner, inner, unroll=7)
    own = xs[0]
    norm = jnp.sum(fold_rows(own * own), axis=0, keepdims=True)
    inner = jnp.sum(inner, axis=0, keepdims=True)
    row_ids = lax.broadcasted_iota(jnp.int32, (8, B), 0)
    v_out[...] = jnp.where(row_ids == 0, inner, jnp.where(row_ids == 1, norm, 0.0))
    for k in range(15, 0, -1):
        remote(v_out, v_near.at[k - 1], sent.at[8], sum_recv.at[0], near(k)).start()
    last = 16 - 16 * par
    i = 7 - 7 * par
    arrive(cross_in.at[i], back_recv.at[i])
    part[last] += cross_in[i]
    for e in (1, 3, 2):
        for d in (2, 1, 3):
            q = 3 * (e - 1) + d - 1
            go(6, X_FIRST, part.at[slot(e, d, 0, 0), x_rows], half_a.at[q], half_recv.at[e - 1], at_y(d))
            go(6, B - X_FIRST, part.at[slot(d, e, 0, 0), y_rows], half_b.at[q], half_recv.at[e + 2], at_x(d))
    for c in (14, 2, 12, 4):
        merge(c)
    for c, q in ((14, 1), (2, 0)):
        for h in (0, 1):
            send_near(c, h, q)

    def send_axis(c, rows, dst, device):
        go(7, rows.size, part.at[c, rows], dst, end_recv.at[1], device)

    for e in (1, 3, 2):
        send_axis(slot(e, 0, 0, 0), y_rows, axis_high.at[2 + e], at_x(e))
        send_axis(slot(0, e, 0, 0), x_rows, axis_low.at[2 + e], at_y(e))

    arrive(relay_in.at[pl.ds(3, 3)], relay_recv.at[1])
    part[12, half[0]] += relay_in[3]
    part[12, half[1]] += relay_in[4] + relay_in[5]
    for h in (0, 1):
        send_near(12, h, 3)
    arrive(relay_in.at[pl.ds(0, 3)], relay_recv.at[0])
    part[4, half[0]] += relay_in[0] + relay_in[2]
    part[4, half[1]] += relay_in[1]
    for h in (0, 1):
        send_near(4, h, 2)

    arrive(v_near, sum_recv.at[0])
    mid = v_out[...]
    for k in range(15):
        mid = mid + v_near[k]
    v_mid[...] = mid
    for k in range(1, 16):
        remote(v_mid, v_far.at[k - 1], sent.at[9], sum_recv.at[1], near(16 * k)).start()

    for e in (1, 3, 2):
        at = slot(e, 0, 0, 0)
        q = 3 * (e - 1)
        arrive(half_a.at[pl.ds(q, 3)], half_recv.at[e - 1])
        part[at, x_rows] += half_a[q] + half_a[q + 1] + half_a[q + 2]
        send_axis(at, x_rows, axis_low.at[e - 1], at_x(e))
        at = slot(0, e, 0, 0)
        arrive(half_b.at[pl.ds(q, 3)], half_recv.at[e + 2])
        part[at, y_rows] += half_b[q] + half_b[q + 1] + half_b[q + 2]
        send_axis(at, y_rows, axis_high.at[e - 1], at_y(e))

    arrive(near_in, end_recv.at[0])
    arrive(xs.at[pl.ds(0, 6)], end_recv.at[1])
    low = part[0, 0:HALF]
    high = part[0, HALF:B]
    for q in range(4):
        low = low + near_in[2 * q]
        high = high + near_in[2 * q + 1]
    image_ref[0:HALF] = low
    image_ref[HALF:B] = high
    low = image_ref[0:X_FIRST]
    high = image_ref[X_FIRST:B]
    for q in range(6):
        low = low + axis_low[q]
        high = high + axis_high[q]
    image_ref[0:X_FIRST] = low
    image_ref[X_FIRST:B] = high
    arrive(v_far, sum_recv.at[1])
    total = v_mid[...]
    for k in range(15):
        total = total + v_far[k]
    step_ref[...] = jnp.broadcast_to(total[1:2] / total[0:1], (8, B))
    for group, rows in enumerate(rows_sent):
        whole = tf.at[pl.ds(0, rows // B)]
        remote(whole, whole, sent.at[group], block_recv, partner).wait_send()
    remote(v_near, v_near, sent.at[8], block_recv, partner).wait_send()
    remote(v_near, v_near, sent.at[9], block_recv, partner).wait_send()


def update_kernel(x_ref, image_ref, step_ref, sol_ref, res_ref):
    own = x_ref[...]
    step = step_ref[0:1]
    sol_ref[...] = step * own
    res_ref[...] = own - step * image_ref[...]


def per_device(right_side, kernel_tiles, route_pairs):
    vmem = pltpu.VMEM
    dma = pltpu.SemaphoreType.DMA
    sems = [dma((10,)), dma((10,)), dma((6,)), dma(()), dma(()), dma(()), dma((8,)), dma((2,)), dma((6,)), dma((2,)), dma((2,))]
    block = jax.ShapeDtypeStruct((B, B), F32)
    whole = pl.BlockSpec(memory_space=vmem)
    image, step = pl.pallas_call(
        cg_kernel,
        out_shape=(block, jax.ShapeDtypeStruct((8, B), F32)),
        in_specs=[pl.BlockSpec(memory_space=pl.ANY)] * 3,
        out_specs=(whole, whole),
        scratch_shapes=[
            pltpu.SMEM((2, NT), jnp.int32),
            vmem((NT, B, B), F32),
            vmem((NT, 2, B, 2 * B), BF16),
            vmem((NC, B, B), F32),
            vmem((NC, 2 * B, 2 * B), BF16),
            vmem((NC, B, B), F32),
            vmem((16, B, B), F32),
            vmem((31, B, B), F32),
            vmem((16, B, B), F32),
            vmem((32, B, B), F32),
            vmem((8, B, B), F32),
            vmem((6, HALF, B), F32),
            vmem((8, HALF, B), F32),
            vmem((6, X_FIRST, B), F32),
            vmem((6, B - X_FIRST, B), F32),
            vmem((9, X_FIRST, B), F32),
            vmem((9, B - X_FIRST, B), F32),
            vmem((8, B), F32),
            vmem((8, B), F32),
            vmem((15, 8, B), F32),
            vmem((15, 8, B), F32),
            pltpu.SMEM((16,), jnp.int32),
            pltpu.SMEM((32,), jnp.int32),
            pltpu.SMEM((NC,), jnp.int32),
            pltpu.SMEM((NC,), jnp.int32),
            dma((CHUNKS,)),
            dma(()),
            dma(()),
        ]
        + sems,
        compiler_params=pltpu.CompilerParams(
            collective_id=0, has_side_effects=True, vmem_limit_bytes=60 * 1024 * 1024
        ),
    )(route_pairs.T, right_side, kernel_tiles)
    return pl.pallas_call(
        update_kernel,
        out_shape=(block, block),
        in_specs=[whole, whole, whole],
        out_specs=(whole, whole),
    )(right_side, image, step)


def solution(mesh):
    return jax.shard_map(
        per_device,
        mesh=mesh,
        in_specs=(P("blk", None), P("blk", None, None, None), P()),
        out_specs=(P("blk", None), P("blk", None)),
        check_vma=False,
    )
```

```python
import functools

import jax
import jax.numpy as jnp
from jax import lax
from jax.experimental import pallas as pl
from jax.experimental.pallas import tpu as pltpu
from jax.sharding import PartitionSpec as P

MESH = pl.DeviceIdType.MESH
NB = 256
B = 128
NT = 129
NC = 31
CHUNK = 16
CHUNKS = 9
HALF = B // 2
X_FIRST = 64
F32 = jnp.float32
BF16 = jnp.bfloat16


def split_pair(value):
    high = value.astype(BF16)
    low = (value - high.astype(F32)).astype(BF16)
    return high, low


def sort_network(count):
    pairs = []
    p = 1
    while p < count:
        k = p
        while k >= 1:
            for j in range(k % p, count - k, 2 * k):
                for i in range(min(k, count - j - k)):
                    if (i + j) // (2 * p) == (i + j + k) // (2 * p):
                        pairs.append((i + j, i + j + k))
            k //= 2
        p *= 2
    return pairs


def cg_kernel(
    pairs_hbm, x_hbm, tiles, image_ref, step_ref,
    rp,
    tf, tb, xs, wb, part, wide, tight, wide_runs, tight_runs,
    cross_in, relay_in, near_in, axis_low, axis_high, half_a, half_b,
    v_out, v_mid, v_near, v_far, wide_keys, tight_keys, wide_last, tight_last,
    tile_sem, own_sem, pairs_sem, sent, g_recv, first_recv, early_recv, block_recv, cross_recv, back_recv, relay_recv, half_recv, end_recv, sum_recv,
):
    me = lax.axis_index("blk")
    par = lax.rem(me, 2)
    partner = me + 1 - 2 * par
    col = me // 16
    px = me // 64
    py = lax.rem(col, 4)

    def near(step):
        return lax.rem(me + step + NB, NB)

    def at_x(step):
        return me + (lax.rem(px + step, 4) - px) * 64

    def at_y(step):
        return me + (lax.rem(py + step, 4) - py) * 16

    def slot(dx, dy, tx, ty):
        owner_col = lax.rem(px + dx, 4) * 4 + lax.rem(py + dy, 4)
        there_col = lax.rem(px + tx, 4) * 4 + lax.rem(py + ty, 4)
        return 15 + lax.rem(owner_col - there_col + 16, 16)

    def remote(src, dst, send_sem, recv_sem, device):
        return pltpu.make_async_remote_copy(
            src_ref=src, dst_ref=dst, send_sem=send_sem, recv_sem=recv_sem,
            device_id=(device,), device_id_type=MESH,
        )

    def arrive(dst, recv_sem):
        remote(dst, dst, sent.at[0], recv_sem, partner).wait_recv()

    half = [pl.ds(0, HALF), pl.ds(HALF, HALF)]
    x_rows, y_rows = pl.ds(0, X_FIRST), pl.ds(X_FIRST, B - X_FIRST)
    rows_sent = [0] * 8

    def go(group, rows, src, dst, recv_sem, device):
        rows_sent[group] += rows
        remote(src, dst, sent.at[group], recv_sem, device).start()

    own_copy = pltpu.make_async_copy(x_hbm, xs.at[0], own_sem)
    own_copy.start()
    pairs_copy = pltpu.make_async_copy(pairs_hbm, rp, pairs_sem)
    pairs_copy.start()

    def tile_copy(q, count):
        span = pl.ds(q * CHUNK, count)
        return pltpu.make_async_copy(tiles.at[0, span], tf.at[span], tile_sem.at[q])


    barrier = pltpu.get_barrier_semaphore()
    axis_devices = [at_x(d) for d in (1, 2, 3)] + [at_y(d) for d in (1, 2, 3)]
    for device in axis_devices + [near(2), near(4), near(12), near(14), near(-2), near(-4), partner]:
        pl.semaphore_signal(barrier, inc=1, device_id=(device,), device_id_type=MESH)
    own_copy.wait()
    pl.semaphore_wait(barrier, 13)

    def own_to_x(d, rows, sem):
        go(0, rows.size, xs.at[0, rows], xs.at[slot(0, 0, d, 0), rows], sem, at_x(d))

    def own_to_y(d, rows, sem):
        go(0, rows.size, xs.at[0, rows], xs.at[slot(0, 0, 0, d), rows], sem, at_y(d))

    for h in (0, 1):
        go(1, HALF, xs.at[0, half[1 - h]], xs.at[12, half[1 - h]], g_recv.at[3 - h], near(-12))
        go(1, HALF, xs.at[0, half[h]], xs.at[4, half[h]], g_recv.at[h], near(-4))
    for d in (2, 1, 3):
        own_to_x(d, x_rows, first_recv.at[d - 1])
        own_to_y(d, y_rows, first_recv.at[2 + d])
    go(1, B, xs.at[0], xs.at[2], g_recv.at[4], near(-2))
    go(1, B, xs.at[0], xs.at[14], g_recv.at[5], near(-14))
    for q in range(CHUNKS - 1):
        tile_copy(q, CHUNK).start()
    tile_copy(CHUNKS - 1, 1).start()

    def ordered(keys, count):
        keys = list(keys)
        for lower, upper in sort_network(count):
            if upper < len(keys):
                small, big = jnp.minimum(keys[lower], keys[upper]), jnp.maximum(keys[lower], keys[upper])
                keys[lower], keys[upper] = small, big
        return keys

    pairs_copy.wait()
    keys = [rp[0, 16 * m] * 32 + m - 1 for m in range(1, 9)]
    keys += [rp[1, 16 * m] * 32 + m + 7 for m in range(1, 8)]
    for i, key in enumerate(ordered(keys, 16)):
        wide_keys[i] = key
    keys = [rp[0, t] * 32 + t for t in range(16)] + [rp[1, t] * 32 + t + 15 for t in range(1, 16)]
    for i, key in enumerate(ordered(keys, 32)):
        tight_keys[i] = key

    def find_last(c, carry):
        for keys, last, count in ((wide_keys, wide_last, 15), (tight_keys, tight_last, 31)):
            found = jnp.int32(-1)
            for i in range(count):
                found = found + (keys[i] < (c + 1) * 32).astype(jnp.int32)
            ends_here = lax.div(keys[jnp.maximum(found, 0)], 32) == c
            last[c] = jnp.where(ends_here, found, count)
        return carry

    lax.fori_loop(0, NC, find_last, 0)


    def split_tile(t):
        high, low = split_pair(tf[t])
        tb[t, 0, :, 0:B] = high
        tb[t, 0, :, B : 2 * B] = low
        tb[t, 1, :, 0:B] = high.T
        tb[t, 1, :, B : 2 * B] = low.T

    def prepare(q, carry):
        tile_copy(q, CHUNK).wait()
        for u in range(CHUNK):
            split_tile(q * CHUNK + u)
        return carry

    def cross(r):
        go(2, B, xs.at[r], xs.at[r - 1 + 2 * par], cross_recv, partner)

    def forward(e):
        src = slot(e, 0, 0, 0)
        arrive(xs.at[src, x_rows], first_recv.at[3 - e])
        for d in (2, 1, 3):
            sem = early_recv if (e, d) == (1, 3) else block_recv
            go(3, X_FIRST, xs.at[src, x_rows], xs.at[slot(e, 0, 0, d), x_rows], sem, at_y(d))
        src = slot(0, e, 0, 0)
        arrive(xs.at[src, y_rows], first_recv.at[6 - e])
        for d in (2, 1, 3):
            sem = early_recv if (e, d) == (1, 3) else block_recv
            go(3, B - X_FIRST, xs.at[src, y_rows], xs.at[slot(0, e, d, 0), y_rows], sem, at_x(d))

    def forward_4(h):
        arrive(xs.at[4, half[h]], g_recv.at[h])
        if h == 0:
            go(1, HALF, xs.at[4, half[0]], xs.at[8, half[0]], g_recv.at[6], near(-4))
        go(1, HALF, xs.at[4, half[h]], xs.at[6, half[h]], g_recv.at[7], near(-2))

    def forward_12(h):
        arrive(xs.at[12, half[h]], g_recv.at[2 + h])
        if h == 1:
            go(1, HALF, xs.at[12, half[1]], xs.at[8, half[1]], g_recv.at[9], near(4))
        go(1, HALF, xs.at[12, half[h]], xs.at[10, half[h]], g_recv.at[8], near(2))

    forward(3)
    forward_4(0)
    forward(1)
    forward_4(1)
    forward_12(1)
    forward_12(0)
    for d in (3, 1, 2):
        own_to_y(d, x_rows, early_recv if d == 3 else block_recv)
        own_to_x(d, y_rows, block_recv)
    lax.fori_loop(0, 3, prepare, 0)
    forward(2)
    lax.fori_loop(3, CHUNKS - 1, prepare, 0)
    tile_copy(CHUNKS - 1, 1).wait()
    split_tile(NT - 1)
    for r in (4, 12):
        cross(r)
    for r, q in ((2, 4), (14, 5)):
        arrive(xs.at[r], g_recv.at[q])
        cross(r)

    def split_block(c, carry):
        high, low = split_pair(xs[c])
        wb[c, 0:B, 0:B] = high
        wb[c, 0:B, B : 2 * B] = low
        wb[c, B : 2 * B, 0:B] = high
        wb[c, B : 2 * B, B : 2 * B] = low
        return carry

    def product(t, turn, c):
        both = jnp.dot(tb[t, turn], wb[c], preferred_element_type=F32)
        return both[:, 0:B] + both[:, B : 2 * B]

    def as_mask(flag):
        return flag.astype(jnp.int32).astype(F32)

    zero = jnp.zeros((B, B), F32)

    def run_sums(keys, products, runs, count):
        total = zero
        for i in range(count):
            key = keys[i]
            before = keys[max(i - 1, 0)]
            total = as_mask(lax.div(before, 32) == lax.div(key, 32)) * total + products[lax.rem(key, 32)]
            runs[i] = total
        runs[count] = zero

    def orient(t, j, k):
        ahead = rp[0, t] == j
        small = jnp.where(ahead, j, 16 - j)
        large = jnp.where(ahead, 15 + k, 32 - k)
        return jnp.where(ahead, 0, 1), small, large, as_mask(ahead)

    def one_to_small(j):
        first, second = zero, zero
        for k in range(2, 9):
            turn, _, large, mask = orient(16 * k - j, j, k)
            value = product(16 * k - j, turn, large)
            first = first + mask * value
            second = second + (1.0 - mask) * value
        return first, second

    def far_to_small(j):
        first, second = one_to_small(j)
        third, fourth = one_to_small(16 - j)
        part[j] = first + fourth
        part[16 - j] = second + third

    def small_pair(i, carry):
        far_to_small(2 * i + 1)
        far_to_small(2 * i + 2)
        return carry

    def far_to_large(k):
        first, second = zero, zero
        for j in range(1, 16):
            turn, small, _, mask = orient(16 * k - j, j, k)
            value = product(16 * k - j, 1 - turn, small)
            first = first + mask * value
            second = second + (1.0 - mask) * value
        part[15 + k] = first
        part[32 - k] = second

    def large_pair(i, carry):
        far_to_large(2 * i + 1)
        far_to_large(2 * i + 2)
        return carry

    def add_runs(c, carry):
        part[c] += wide_runs[wide_last[c]] + tight_runs[tight_last[c]]
        return carry

    for r, q in ((6, 7), (10, 8)):
        arrive(xs.at[r], g_recv.at[q])
        cross(r)
    arrive(xs.at[pl.ds(0, 12), pl.ds(0, 16)], early_recv)
    go(2, B, xs.at[16 - 16 * par], xs.at[15 - 14 * par], cross_recv, partner)
    arrive(xs.at[pl.ds(0, 21), y_rows], block_recv)
    split_block(0, 0)
    lax.fori_loop(16, NC, split_block, 0, unroll=5)
    for m in range(1, 9):
        wide[m - 1] = product(16 * m, 0, rp[1, 16 * m])
        if m < 8:
            wide[m + 7] = product(16 * m, 1, rp[0, 16 * m])
    run_sums(wide_keys, wide, wide_runs, 15)
    arrive(xs.at[8, half[0]], g_recv.at[6])
    arrive(xs.at[8, half[1]], g_recv.at[9])
    cross(8)
    lax.fori_loop(0, 2, small_pair, 0)
    lax.fori_loop(2, 3, small_pair, 0)
    far_to_small(7)
    first, second = one_to_small(8)
    part[8] = first + second

    arrive(xs.at[pl.ds(1, 8)], cross_recv)
    lax.fori_loop(1, 16, split_block, 0, unroll=5)
    for t in range(16):
        tight[t] = product(t, 0, rp[1, t])
        if t > 0:
            tight[t + 15] = product(t, 1, rp[0, t])
    run_sums(tight_keys, tight, tight_runs, 31)

    def cross_back(i):
        go(4, B, part.at[2 * i + 1], cross_in.at[i], back_recv.at[i], partner)

    def finish_small(c, carry):
        part[c] += tight_runs[tight_last[c]]
        return carry

    lax.fori_loop(1, 16, finish_small, 0, unroll=5)
    for i in (3, 4, 2, 5, 1, 6, 0, 7):
        cross_back(i)
    part[0] = wide_runs[wide_last[0]] + tight_runs[tight_last[0]]
    part[16] = wide_runs[wide_last[16]] + tight_runs[tight_last[16]]

    def fold_rows(value):
        total = value[0:8]
        for q in range(1, B // 8):
            total = total + value[8 * q : 8 * q + 8]
        return total

    def add_inner(c, carry):
        return carry + fold_rows(xs[c] * part[c])

    inner = lax.fori_loop(0, 17, add_inner, jnp.zeros((8, B), F32), unroll=6)

    def merge(c):
        i = c // 2 - 1 + par
        arrive(cross_in.at[i], back_recv.at[i])
        part[c] += cross_in[i]

    def send_near(c, h, q):
        go(5, HALF, part.at[c, half[h]], near_in.at[2 * q + h], end_recv.at[0], near(c))

    far_to_large(2)
    for c in (8, 6, 10):
        merge(c)
    def send_relay(c, h, q, device):
        go(5, HALF, part.at[c, half[h]], relay_in.at[q], relay_recv.at[q // 3], device)

    send_relay(8, 0, 2, near(4))
    send_relay(8, 1, 5, near(-4))
    for h in (0, 1):
        send_relay(6, h, h, near(2))
        send_relay(10, h, 3 + h, near(-2))
    lax.fori_loop(1, 4, large_pair, 0)
    lax.fori_loop(17, NC, add_runs, 0, unroll=7)
    inner = lax.fori_loop(17, NC, add_inner, inner, unroll=7)
    own = xs[0]
    norm = jnp.sum(fold_rows(own * own), axis=0, keepdims=True)
    inner = jnp.sum(inner, axis=0, keepdims=True)
    row_ids = lax.broadcasted_iota(jnp.int32, (8, B), 0)
    v_out[...] = jnp.where(row_ids == 0, inner, jnp.where(row_ids == 1, norm, 0.0))
    for k in range(15, 0, -1):
        remote(v_out, v_near.at[k - 1], sent.at[8], sum_recv.at[0], near(k)).start()
    last = 16 - 16 * par
    i = 7 - 7 * par
    arrive(cross_in.at[i], back_recv.at[i])
    part[last] += cross_in[i]
    for e in (1, 3, 2):
        for d in (2, 1, 3):
            q = 3 * (e - 1) + d - 1
            go(6, X_FIRST, part.at[slot(e, d, 0, 0), x_rows], half_a.at[q], half_recv.at[e - 1], at_y(d))
            go(6, B - X_FIRST, part.at[slot(d, e, 0, 0), y_rows], half_b.at[q], half_recv.at[e + 2], at_x(d))
    for c in (14, 2, 12, 4):
        merge(c)
    for c, q in ((14, 1), (2, 0)):
        for h in (0, 1):
            send_near(c, h, q)

    def send_axis(c, rows, dst, device):
        go(7, rows.size, part.at[c, rows], dst, end_recv.at[1], device)

    for e in (1, 3, 2):
        send_axis(slot(e, 0, 0, 0), y_rows, axis_high.at[2 + e], at_x(e))
        send_axis(slot(0, e, 0, 0), x_rows, axis_low.at[2 + e], at_y(e))

    arrive(relay_in.at[pl.ds(3, 3)], relay_recv.at[1])
    part[12, half[0]] += relay_in[3]
    part[12, half[1]] += relay_in[4] + relay_in[5]
    for h in (0, 1):
        send_near(12, h, 3)
    arrive(relay_in.at[pl.ds(0, 3)], relay_recv.at[0])
    part[4, half[0]] += relay_in[0] + relay_in[2]
    part[4, half[1]] += relay_in[1]
    for h in (0, 1):
        send_near(4, h, 2)

    arrive(v_near, sum_recv.at[0])
    mid = v_out[...]
    for k in range(15):
        mid = mid + v_near[k]
    v_mid[...] = mid
    for k in range(1, 16):
        remote(v_mid, v_far.at[k - 1], sent.at[9], sum_recv.at[1], near(16 * k)).start()

    for e in (1, 3, 2):
        at = slot(e, 0, 0, 0)
        q = 3 * (e - 1)
        arrive(half_a.at[pl.ds(q, 3)], half_recv.at[e - 1])
        part[at, x_rows] += half_a[q] + half_a[q + 1] + half_a[q + 2]
        send_axis(at, x_rows, axis_low.at[e - 1], at_x(e))
        at = slot(0, e, 0, 0)
        arrive(half_b.at[pl.ds(q, 3)], half_recv.at[e + 2])
        part[at, y_rows] += half_b[q] + half_b[q + 1] + half_b[q + 2]
        send_axis(at, y_rows, axis_high.at[e - 1], at_y(e))

    arrive(near_in, end_recv.at[0])
    arrive(xs.at[pl.ds(0, 6)], end_recv.at[1])
    low = part[0, 0:HALF]
    high = part[0, HALF:B]
    for q in range(4):
        low = low + near_in[2 * q]
        high = high + near_in[2 * q + 1]
    image_ref[0:HALF] = low
    image_ref[HALF:B] = high
    low = image_ref[0:X_FIRST]
    high = image_ref[X_FIRST:B]
    for q in range(6):
        low = low + axis_low[q]
        high = high + axis_high[q]
    image_ref[0:X_FIRST] = low
    image_ref[X_FIRST:B] = high
    arrive(v_far, sum_recv.at[1])
    total = v_mid[...]
    for k in range(15):
        total = total + v_far[k]
    step_ref[...] = jnp.broadcast_to(total[1:2] / total[0:1], (8, B))
    for group, rows in enumerate(rows_sent):
        whole = tf.at[pl.ds(0, rows // B)]
        remote(whole, whole, sent.at[group], block_recv, partner).wait_send()
    remote(v_near, v_near, sent.at[8], block_recv, partner).wait_send()
    remote(v_near, v_near, sent.at[9], block_recv, partner).wait_send()


def update_kernel(x_ref, image_ref, step_ref, sol_ref, res_ref):
    own = x_ref[...]
    step = step_ref[0:1]
    sol_ref[...] = step * own
    res_ref[...] = own - step * image_ref[...]


def per_device(right_side, kernel_tiles, route_pairs):
    vmem = pltpu.VMEM
    dma = pltpu.SemaphoreType.DMA
    sems = [dma((10,)), dma((10,)), dma((6,)), dma(()), dma(()), dma(()), dma((8,)), dma((2,)), dma((6,)), dma((2,)), dma((2,))]
    block = jax.ShapeDtypeStruct((B, B), F32)
    whole = pl.BlockSpec(memory_space=vmem)
    image, step = pl.pallas_call(
        cg_kernel,
        out_shape=(block, jax.ShapeDtypeStruct((8, B), F32)),
        in_specs=[pl.BlockSpec(memory_space=pl.ANY)] * 3,
        out_specs=(whole, whole),
        scratch_shapes=[
            pltpu.SMEM((2, NT), jnp.int32),
            vmem((NT, B, B), F32),
            vmem((NT, 2, B, 2 * B), BF16),
            vmem((NC, B, B), F32),
            vmem((NC, 2 * B, 2 * B), BF16),
            vmem((NC, B, B), F32),
            vmem((16, B, B), F32),
            vmem((31, B, B), F32),
            vmem((16, B, B), F32),
            vmem((32, B, B), F32),
            vmem((8, B, B), F32),
            vmem((6, HALF, B), F32),
            vmem((8, HALF, B), F32),
            vmem((6, X_FIRST, B), F32),
            vmem((6, B - X_FIRST, B), F32),
            vmem((9, X_FIRST, B), F32),
            vmem((9, B - X_FIRST, B), F32),
            vmem((8, B), F32),
            vmem((8, B), F32),
            vmem((15, 8, B), F32),
            vmem((15, 8, B), F32),
            pltpu.SMEM((16,), jnp.int32),
            pltpu.SMEM((32,), jnp.int32),
            pltpu.SMEM((NC,), jnp.int32),
            pltpu.SMEM((NC,), jnp.int32),
            dma((CHUNKS,)),
            dma(()),
            dma(()),
        ]
        + sems,
        compiler_params=pltpu.CompilerParams(
            collective_id=0, has_side_effects=True, vmem_limit_bytes=60 * 1024 * 1024
        ),
    )(route_pairs.T, right_side, kernel_tiles)
    return pl.pallas_call(
        update_kernel,
        out_shape=(block, block),
        in_specs=[whole, whole, whole],
        out_specs=(whole, whole),
    )(right_side, image, step)


def solution(mesh):
    return jax.shard_map(
        per_device,
        mesh=mesh,
        in_specs=(P("blk", None), P("blk", None, None, None), P()),
        out_specs=(P("blk", None), P("blk", None)),
        check_vma=False,
    )
```
